32 devices in a mesh: zone: 8 (over z, y), band: 4 (over x, core).
Axes of the slice: x: 2, y: 2, z: 4, core: 2. Of those that a mesh axis runs over, the one named last changes fastest.
Arguments:
- pixels: float32 [4096, 32, 128], P(('zone', 'band')), may hold values from -6 to 6
- inv_var: float32 [4096, 32, 128], P(('zone', 'band')), may hold values from 0.25 to 4
- tile_offset: float32 [2, 4096], P(None, ('zone', 'band')), may hold values from 12 to 116, as said below
- psf_amp: float32 [3, 4096], P(None, ('zone', 'band')), may hold values from 0.3 to 1
- psf_sigma: float32 [3, 4096], P(None, ('zone', 'band')), may hold values from 0.9 to 2
- tile_blob: int32 [4096], P(('zone', 'band')), may hold values from 0 to 511, as said below
- tile_band: int32 [4096], P(('zone', 'band')), may hold values from 0 to 2
- source_pos: float32 [2, 4096], P(None, 'zone'), may hold values from -5.3 to 5.3
- edge_rows: int32 [1024], P('zone'), may hold values from 0 to 511, as said below
- blob_members: int32 [512, 16], P('zone'), may hold values from 0 to 639, as said below
- sources_per_blob: int32 [512], P('zone'), may hold values from 1 to 16, as said below
Outputs:
- fluxes: float32 [3, 4096], P(None, 'zone')
The draws below stay inside these ranges and needn't reach their ends.
Inputs may be any that keep to these rules, and one draw needn't show every extreme that they name: `tile_blob`: blob b lies in zone b // 64. Of one device's 128 tiles at most 32 cover blobs of one zone, and in every draw some zone receives exactly 32 tiles from every device of each band group. `edge_rows`: per zone, 64 lower edge rows then 64 upper edge rows, local row numbers, all 128 distinct. `blob_members`: slots at or beyond the blob's count hold 0. Every source is the live member of exactly one blob: a zone's lower edge rows belong to blobs of the previous zone and its upper edge rows to blobs of the next zone, except the first zone's lower and the last zone's upper rows, which stay in their own zone; the first zone never names the first 64 entries, the last zone never the last 64. `sources_per_blob`: the counts of one zone sum to 512; in every zone some blob has 16. `tile_offset`: row offsets lie within 12 to 20.
All inputs are finite; a program needn't handle non-finite values.
Results may differ from the reference program's by a relative error of at most 0.0003.
Values sent between devices are 32-bit elements; how exact they have to be, the bound alone decides.
A program may use at most 64 MiB of HBM per device.

```python
import math
import jax
import jax.numpy as jnp
from jax import lax

FILTER_BANDS = 3
COMPS = 3
MAX_SOURCES = 16
PH = 32
PW = 128
SRC_DEV = 512
TILE_DEV = 128
BLOB_DEV = 64
EDGE = 64
CAP = 32
TILES = 4096
N_ZONE = 8
N_BAND = 4


def layout(key):
    key = jax.random.fold_in(key, 31)
    key_edge, key_claim, key_full, key_cells = jax.random.split(key, 4)
    extent = SRC_DEV + 2 * EDGE
    zone_ids = jnp.arange(N_ZONE, dtype=jnp.int32)
    edge_lists = jax.vmap(lambda sub_key: jax.random.permutation(sub_key, SRC_DEV)[:2 * EDGE])(jax.random.split(key_edge, N_ZONE)).astype(jnp.int32)
    lower_rows = edge_lists[:, :EDGE]
    upper_rows = edge_lists[:, EDGE:]

    def one_zone(zone_id, lower_list, upper_list, claim_key, full_key, cells_key):
        own_flags = jnp.ones((SRC_DEV,), jnp.int32)
        own_flags = own_flags.at[lower_list].set(jnp.where(zone_id > 0, 0, 1))
        own_flags = own_flags.at[upper_list].set(jnp.where(zone_id < N_ZONE - 1, 0, 1))
        before_flags = jnp.full((EDGE,), jnp.where(zone_id > 0, 1, 0), jnp.int32)
        after_flags = jnp.full((EDGE,), jnp.where(zone_id < N_ZONE - 1, 1, 0), jnp.int32)
        claimed = jnp.concatenate([before_flags, own_flags, after_flags])
        shuffle = jax.random.permutation(claim_key, extent).astype(jnp.int32)
        ranking = jnp.where(claimed == 1, shuffle, shuffle + extent)
        claim_order = jnp.argsort(ranking).astype(jnp.int32)
        cell_total = BLOB_DEV * (MAX_SOURCES - 1)
        full_blob = jax.random.randint(full_key, (), 0, BLOB_DEV)
        cell_shuffle = jax.random.permutation(cells_key, cell_total).astype(jnp.int32)
        cell_blob = jnp.arange(cell_total, dtype=jnp.int32) // (MAX_SOURCES - 1)
        cell_score = jnp.where(cell_blob == full_blob, cell_shuffle - cell_total, cell_shuffle)
        cell_rank = jnp.argsort(jnp.argsort(cell_score)).astype(jnp.int32)
        chosen = (cell_rank < SRC_DEV - BLOB_DEV).astype(jnp.int32)
        counts = 1 + jnp.sum(chosen.reshape(BLOB_DEV, MAX_SOURCES - 1), axis=1)
        starts = jnp.cumsum(counts) - counts
        slot_ids = jnp.arange(MAX_SOURCES, dtype=jnp.int32)
        live_slots = slot_ids[None, :] < counts[:, None]
        picks = jnp.clip(starts[:, None] + slot_ids[None, :], 0, SRC_DEV - 1)
        members = jnp.where(live_slots, claim_order[picks], 0).astype(jnp.int32)
        slot_table = jnp.broadcast_to(slot_ids[None, :], members.shape)
        slot_of = jnp.zeros((extent,), jnp.int32).at[jnp.where(live_slots, members, extent)].set(slot_table, mode='drop')
        return (members, counts.astype(jnp.int32), slot_of)
    members, counts, slot_of = jax.vmap(one_zone)(zone_ids, lower_rows, upper_rows, jax.random.split(key_claim, N_ZONE), jax.random.split(key_full, N_ZONE), jax.random.split(key_cells, N_ZONE))
    own_slots = slot_of[:, EDGE:EDGE + SRC_DEV]
    next_parts = slot_of[:, EDGE + SRC_DEV:]
    prev_parts = slot_of[:, :EDGE]
    lower_values = jnp.concatenate([next_parts[:1], next_parts[:-1]], axis=0)
    upper_values = jnp.concatenate([prev_parts[1:], prev_parts[-1:]], axis=0)

    def place(slots, lower_list, upper_list, lower_vals, upper_vals, zone_id):
        slots = slots.at[lower_list].set(jnp.where(zone_id > 0, lower_vals, slots[lower_list]))
        slots = slots.at[upper_list].set(jnp.where(zone_id < N_ZONE - 1, upper_vals, slots[upper_list]))
        return slots
    source_slots = jax.vmap(place)(own_slots, lower_rows, upper_rows, lower_values, upper_values, zone_ids)
    return (edge_lists, members, counts, source_slots)


def draw_edge_rows(key, part):
    return layout(key)[0].reshape(-1)


def draw_blob_members(key, part):
    return layout(key)[1].reshape(-1, MAX_SOURCES)


def draw_sources_per_blob(key, part):
    return layout(key)[2].reshape(-1)


def draw_source_pos(key, part):
    source_slots = layout(key)[3]
    jitter_key = jax.random.fold_in(key, 57)
    jitter_reach = 0.5
    jitter_noise = jax.random.uniform(jitter_key, (2, N_ZONE * SRC_DEV), jnp.float32, -jitter_reach, jitter_reach)
    flat_slots = source_slots.reshape(-1)
    lattice_row = (flat_slots // 4).astype(jnp.float32) * 3.0 - 4.5
    lattice_col = (flat_slots % 4).astype(jnp.float32) * 3.0 - 4.5
    return jnp.stack([lattice_row, lattice_col]) + jitter_noise


def draw_tile_offset(key, part):
    key = jax.random.fold_in(key, 97)
    row_key, col_key = jax.random.split(key)
    offset_rows = jax.random.uniform(row_key, (TILES,), jnp.float32, 12.0, 20.0)
    offset_cols = jax.random.uniform(col_key, (TILES,), jnp.float32, 12.0, PW - 12.0)
    return jnp.stack([offset_rows, offset_cols])


def draw_tile_blob(key, part):
    key = jax.random.fold_in(key, 83)
    key_busy, key_slots, key_order, key_local = jax.random.split(key, 4)
    holders = N_ZONE * N_BAND
    busy_zone = jax.random.randint(key_busy, (), 0, N_ZONE)
    free_slots = (N_ZONE - 1) * CAP
    picked = jax.vmap(lambda sub_key: jax.random.permutation(sub_key, free_slots)[:TILE_DEV - CAP])(jax.random.split(key_slots, holders))
    other_zone = (busy_zone + 1 + picked // CAP) % N_ZONE
    zone_list = jnp.concatenate([jnp.full((holders, CAP), busy_zone, jnp.int32), other_zone.astype(jnp.int32)], axis=1)
    order_perm = jax.vmap(lambda sub_key: jax.random.permutation(sub_key, TILE_DEV))(jax.random.split(key_order, holders))
    zone_list = jnp.take_along_axis(zone_list, order_perm, axis=1)
    local_blob = jax.random.randint(key_local, (holders, TILE_DEV), 0, BLOB_DEV)
    return (zone_list * BLOB_DEV + local_blob).reshape(-1).astype(jnp.int32)


def place_ends(drawn, stream_key, least, high):
    shape = drawn.shape
    spot = [jax.random.randint(jax.random.fold_in(stream_key, axis), (), 0, shape[axis]) for axis in range(len(shape))]
    drawn = drawn.at[tuple(spot)].set(least)
    longest = shape.index(max(shape))
    spot[longest] = (spot[longest] + 1) % shape[longest]
    return drawn.at[tuple(spot)].set(high)


def block_levels(key, shape, shards, smallest, largest):
    level = 1.0
    for dim, parts in shards:
        draws = jax.random.uniform(jax.random.fold_in(jax.random.fold_in(key, 6), dim), (parts,), jnp.float32, smallest / len(shards), largest / len(shards))
        level = level * jnp.repeat(jnp.exp(draws), shape[dim] // parts).reshape((-1,) + (1,) * (len(shape) - 1 - dim))
    return level


def centred(rng, shape, scale, bound, pieces=(), kind=jnp.bfloat16):
    drawn = scale * jax.random.normal(rng, shape, jnp.float32)
    if pieces:
        drawn = drawn * block_levels(rng, shape, pieces, -0.22, 0.18)
    return jnp.clip(drawn, -bound, bound).astype(kind)


def setup_inputs(seed: int = 0) -> dict:
    seeds = jax.random.split(jax.random.key(seed), 12)
    return {
        "pixels": centred(seeds[0], (TILES, PH, PW), 1.0, 6.0, ((0, 32),), jnp.float32),
        "inv_var": jnp.clip(jnp.exp(math.log(4.0) - 2.7725887 * jax.random.uniform(seeds[1], (TILES, PH, PW), jnp.float32) ** block_levels(seeds[1], (TILES, PH, PW), ((0, 32),), -0.2, 0.2)), 0.25, 4.0),
        "tile_offset": draw_tile_offset(jax.random.fold_in(seeds[11], 71), 0),
        "psf_amp": jnp.clip(jnp.exp(math.log(1.0) - 1.2039728 * jax.random.uniform(seeds[3], (COMPS, TILES), jnp.float32) ** block_levels(seeds[3], (COMPS, TILES), ((1, 32),), -0.2, 0.2)), 0.3, 1.0),
        "psf_sigma": jnp.clip(jnp.exp(math.log(2.0) - 0.798507723 * jax.random.uniform(seeds[4], (COMPS, TILES), jnp.float32) ** block_levels(seeds[4], (COMPS, TILES), ((1, 32),), -0.2, 0.2)), 0.9, 2.0),
        "tile_blob": draw_tile_blob(jax.random.fold_in(seeds[11], 71), 0),
        "tile_band": place_ends(jax.random.randint(seeds[6], (TILES,), 0, FILTER_BANDS), jax.random.fold_in(seeds[6], 1), 0, FILTER_BANDS - 1).astype(jnp.int32),
        "source_pos": draw_source_pos(jax.random.fold_in(seeds[11], 71), 0),
        "edge_rows": draw_edge_rows(jax.random.fold_in(seeds[11], 71), 0),
        "blob_members": draw_blob_members(jax.random.fold_in(seeds[11], 71), 0),
        "sources_per_blob": draw_sources_per_blob(jax.random.fold_in(seeds[11], 71), 0),
    }


HIGH = lax.Precision.HIGHEST
PRIOR = 1.0

def terms_per_tile(tile_image_pixels, tile_weight_pixels, pixel_shift, source_amplitude, profile_widths, source_location, slot_alive_flags):
    pixel_rows = jnp.arange(tile_image_pixels.shape[0]).astype(jnp.float32)
    pixel_cols = jnp.arange(tile_image_pixels.shape[1]).astype(jnp.float32)
    inverse_spread = 0.5 / (profile_widths * profile_widths)
    row_displacement = pixel_rows[None, :] - pixel_shift[0] - source_location[0][:, None]
    delta_col = pixel_cols[None, :] - pixel_shift[1] - source_location[1][:, None]
    row_profile = jnp.exp(-inverse_spread[None, :, None] * (row_displacement * row_displacement)[:, None, :]) * (source_amplitude[None, :, None] * slot_alive_flags[:, None, None])
    profile_col = jnp.exp(-inverse_spread[None, :, None] * (delta_col * delta_col)[:, None, :])
    rendered = jnp.sum(row_profile[:, :, :, None] * profile_col[:, :, None, :], axis=1).reshape(row_profile.shape[0], -1)
    weighted = rendered * tile_weight_pixels.reshape(1, -1)
    normal = jnp.einsum('sp,tp->st', weighted, rendered, precision=HIGH)
    projected = jnp.einsum('sp,p->s', weighted, tile_image_pixels.reshape(-1), precision=HIGH)
    return (normal, projected)

def reference(pixels, inv_var, tile_offset, psf_amp, psf_sigma, tile_blob, tile_band, source_pos, edge_rows, blob_members, sources_per_blob):
    blob_total = BLOB_DEV * N_ZONE
    edges = edge_rows.reshape(N_ZONE, 2, EDGE)
    zone_of = (jnp.arange(blob_total, dtype=jnp.int32) // BLOB_DEV)[:, None]
    before_zone = jnp.clip(zone_of - 1, 0, N_ZONE - 1)
    after_zone = jnp.clip(zone_of + 1, 0, N_ZONE - 1)
    from_prev = edges[before_zone, 1, jnp.clip(blob_members, 0, EDGE - 1)] + before_zone * SRC_DEV
    from_own = zone_of * SRC_DEV + jnp.clip(blob_members - EDGE, 0, SRC_DEV - 1)
    from_next = edges[after_zone, 0, jnp.clip(blob_members - EDGE - SRC_DEV, 0, EDGE - 1)] + after_zone * SRC_DEV
    source_of = jnp.where(blob_members < EDGE, from_prev, jnp.where(blob_members < EDGE + SRC_DEV, from_own, from_next)).astype(jnp.int32)
    alive = (jnp.arange(MAX_SOURCES, dtype=jnp.int32)[None, :] < sources_per_blob[:, None]).astype(jnp.float32)
    member_pos = jnp.transpose(source_pos[:, source_of], (1, 0, 2))
    tile_pos = member_pos[tile_blob]
    tile_alive = alive[tile_blob]

    def single_tile(packed):
        return terms_per_tile(*packed)
    normal, projected = lax.map(single_tile, (pixels, inv_var, tile_offset.T, psf_amp.T, psf_sigma.T, tile_pos, tile_alive), batch_size=16)
    target = (tile_blob * FILTER_BANDS + tile_band).astype(jnp.int32)
    normal_total = jax.ops.segment_sum(normal, target, num_segments=blob_total * FILTER_BANDS)
    rhs_total = jax.ops.segment_sum(projected, target, num_segments=blob_total * FILTER_BANDS)
    system = normal_total + PRIOR * jnp.eye(MAX_SOURCES, dtype=jnp.float32)[None, :, :]
    solved_fluxes = jnp.linalg.solve(system, rhs_total[:, :, None])[:, :, 0]
    value_entries = solved_fluxes.reshape(blob_total, FILTER_BANDS, MAX_SOURCES) * alive[:, None, :]
    spread = jnp.transpose(value_entries, (1, 0, 2)).reshape(FILTER_BANDS, -1)
    fluxes = jnp.zeros((FILTER_BANDS, SRC_DEV * N_ZONE), jnp.float32).at[:, source_of.reshape(-1)].add(spread)
    return fluxes
```

```python
import functools
import math

import jax
import jax.numpy as jnp
from jax import lax
from jax.experimental import pallas as pl
from jax.experimental.pallas import tpu as pltpu
from jax.sharding import PartitionSpec as P

FILTER_BANDS = 3
COMPS = 3
SLOTS = 16
HALF = SLOTS // 2
LANES = 128
SEATS = 4
SEAT = LANES // SEATS
TILES_STEP = 16
PRIOR = 1.0
FAR = 1.0e4
LOG2E = math.log2(math.e)

VMEM = pl.BlockSpec(memory_space=pltpu.VMEM)
SMEM = pl.BlockSpec(memory_space=pltpu.SMEM)
ANY = pl.BlockSpec(memory_space=pl.ANY)
MESH = pl.DeviceIdType.MESH


def iota(shape, axis):
    return lax.broadcasted_iota(jnp.int32, shape, axis)


def take(table, index):
    return jnp.take_along_axis(table, index, axis=1, mode="promise_in_bounds")


def spread_rows(row, shape):
    return jnp.broadcast_to(row, shape)


def lookup(rows, index):
    found = jnp.zeros(index.shape, rows[0].dtype)
    low = index & (LANES - 1)
    for part, row in enumerate(rows):
        hit = take(spread_rows(row, index.shape), low)
        found = jnp.where(index // LANES == part, hit, found)
    return found


class Sizes:
    def __init__(self, zones, bands, sources, edge, blobs, tiles):
        self.zones, self.bands = zones, bands
        self.sources, self.edge, self.blobs, self.tiles = sources, edge, blobs, tiles
        self.parts = sources // LANES
        self.member_row = -(-2 * self.parts // 8) * 8
        self.edge_row = self.member_row + HALF
        self.cat_rows = self.edge_row + 8
        self.sent_rows = self.edge_row + 2
        capacity = max(SEATS, (2 * tiles + zones - 1) // zones)
        self.capacity = -(-capacity // SEATS) * SEATS
        self.rest = self.capacity // SEATS
        self.rows = -(-(self.capacity + self.rest) // 8) * 8
        self.share = blobs // bands
        self.systems = FILTER_BANDS * self.share
        self.block = -(-self.systems // 8) * 8
        self.third = self.block // FILTER_BANDS
        self.entries = zones * self.capacity


def catalog_kernel(
    sz, source_ref, edge_ref, member_ref, count_ref, out_ref, pack_ref, send_sem, recv_sem, own_sem
):
    zones = sz.zones
    zone = lax.axis_index("zone")
    band = lax.axis_index("band")
    barrier = pltpu.get_barrier_semaphore()
    targets = [(lax.rem(zone + dz, zones), band) for dz in range(1, zones)]
    for target in targets:
        pl.semaphore_signal(barrier, inc=1, device_id=target, device_id_type=MESH)
    shape = (8, LANES)
    edges = spread_rows(edge_ref[...], shape)
    for coord in range(2):
        rows = []
        for part in range(sz.parts):
            row = source_ref[coord : coord + 1, part * LANES : (part + 1) * LANES]
            pack_ref[coord * sz.parts + part : coord * sz.parts + part + 1, :] = row
            rows.append(row)
        at = sz.edge_row + coord
        pack_ref[at : at + 1, :] = lookup(rows, edges)[:1]
    slot = iota((SLOTS, sz.blobs), 0)
    member = jnp.where(slot < count_ref[...], member_ref[...], -1).astype(jnp.float32)
    pack_ref[sz.member_row : sz.member_row + HALF, :] = jnp.concatenate(
        [member[:HALF], member[HALF:]], axis=1
    )
    sent = pl.ds(0, sz.sent_rows)
    own = pltpu.make_async_copy(pack_ref.at[sent], out_ref.at[zone, sent], own_sem)
    own.start()
    pl.semaphore_wait(barrier, len(targets))
    copies = []
    for order, target in enumerate(targets):
        copy = pltpu.make_async_remote_copy(
            src_ref=pack_ref.at[sent],
            dst_ref=out_ref.at[zone, sent],
            send_sem=send_sem.at[order],
            recv_sem=recv_sem.at[order],
            device_id=target,
            device_id_type=MESH,
        )
        copy.start()
        copies.append(copy)
    own.wait()
    for copy in copies:
        copy.wait()


def resolve_zone(sz, zone, cat_ref, stage_ref, col_ref):
    shape = (HALF, LANES)
    member = cat_ref[zone, sz.member_row : sz.member_row + HALF, :].astype(jnp.int32)
    if isinstance(zone, int):
        before, after = max(zone - 1, 0), min(zone + 1, sz.zones - 1)
    else:
        before, after = jnp.maximum(zone - 1, 0), jnp.minimum(zone + 1, sz.zones - 1)
    low = member < sz.edge
    high = member >= sz.edge + sz.sources
    own = jnp.clip(member - sz.edge, 0, sz.sources - 1)
    rim = jnp.where(
        low, sz.edge + jnp.maximum(member, 0), jnp.where(high, member - sz.edge - sz.sources, 0)
    )
    lane = iota(shape, 1)
    for coord in range(2):
        rows = [
            cat_ref[zone, coord * sz.parts + part : coord * sz.parts + part + 1, :]
            for part in range(sz.parts)
        ]
        at = sz.edge_row + coord
        table = jnp.where(
            lane >= sz.edge,
            spread_rows(cat_ref[before, at : at + 1, :], shape),
            spread_rows(cat_ref[after, at : at + 1, :], shape),
        )
        place = jnp.where(low | high, take(table, rim), lookup(rows, own))
        if coord == 0:
            place = jnp.where(member < 0, FAR, place)
            start = zone * HALF if isinstance(zone, int) else pl.multiple_of(zone * HALF, HALF)
            stage_ref[pl.ds(start, HALF), :] = place
        else:
            col_ref[zone] = place


def spread_zone(sz, zone, turned_ref, row_ref):
    shape = (8, LANES)
    lane = iota(shape, 1)
    per = LANES // HALF
    index = (zone % per) * HALF + lane % HALF
    upper = lane % SLOTS >= HALF
    for part in range(sz.blobs // 8):
        pieces = []
        for half in range(2):
            at = half * sz.blobs + part * 8
            pieces.append(take(turned_ref[zone // per, at : at + 8, :], index))
        start = zone * sz.blobs + part * 8
        if not isinstance(zone, int):
            start = pl.multiple_of(start, 8)
        row_ref[pl.ds(start, 8), :] = jnp.where(upper, pieces[1], pieces[0])


def prepare(sz, cat_ref, shift_ref, amp_ref, sigma_ref, stage_ref, turned_ref, col_ref, row_ref, param_ref):
    each = (lambda body: [body(z) for z in range(sz.zones)]) if sz.zones <= 8 else (
        lambda body: lax.fori_loop(0, sz.zones, lambda z, c: (body(z), c)[1], 0)
    )
    sigma = sigma_ref[...]
    params = jnp.concatenate(
        [(-0.5 * LOG2E) / (sigma * sigma), amp_ref[...], shift_ref[...]], axis=0
    )
    param_ref[:, : params.shape[0]] = params.T
    each(lambda z: resolve_zone(sz, z, cat_ref, stage_ref, col_ref))
    for part in range(turned_ref.shape[0]):
        turned_ref[part] = stage_ref[part * LANES : (part + 1) * LANES, :].T
    each(lambda z: spread_zone(sz, z, turned_ref, row_ref))


def split(value):
    head = value.astype(jnp.bfloat16)
    return head, (value - head.astype(jnp.float32)).astype(jnp.bfloat16)


def tile_kernel(
    sz, blob_ref, band_ref, shift_ref, amp_ref, sigma_ref, cat_ref, pixel_ref, weight_ref,
    out_ref, stage_ref, turned_ref, col_ref, row_ref, param_ref, line_ref, rest_ref, used_ref,
):
    step = pl.program_id(0)
    per, height, _ = pixel_ref.shape

    @pl.when(step == 0)
    def _():
        out_ref[...] = jnp.zeros_like(out_ref)
        rest_ref[...] = jnp.zeros_like(rest_ref)
        for zone in range(sz.zones):
            used_ref[zone] = 0
        prepare(
            sz, cat_ref, shift_ref, amp_ref, sigma_ref,
            stage_ref, turned_ref, col_ref, row_ref, param_ref,
        )

    eight = (HALF, LANES)
    shape = (SLOTS, LANES)
    lane = iota(eight, 1)
    sub = iota(eight, 0)
    sub_f = sub.astype(jnp.float32)
    lane_f = lane.astype(jnp.float32)
    slots_all = COMPS * SLOTS
    width = COMPS * HALF
    keep = (iota(shape, 1) % HALF == iota(shape, 0) % HALF) & (iota(shape, 1) < 3 * width)
    keep = jnp.where(keep, 1.0, 0.0).astype(jnp.bfloat16)
    comp = lane // SLOTS % COMPS
    high_part = (lane < width) | (lane >= 2 * width)
    half_index = lane // HALF % COMPS * SLOTS + lane % HALF
    seat_a = lane // HALF == sub
    seat_b = lane // HALF == sub + HALF
    index_a = (sub + lane % HALF) % SLOTS
    index_b = (sub + HALF + lane % HALF) % SLOTS
    blank = jnp.zeros((LANES - 3 * width, LANES), jnp.float32)
    zero_tail = jnp.zeros((slots_all, LANES), jnp.bfloat16)
    zero_rows = jnp.zeros((LANES - 2 * slots_all, 2 * LANES), jnp.bfloat16)

    for slot in range(per):
        tile = step * per + slot
        blob = blob_ref[tile]
        zone = lax.div(blob, sz.blobs)
        local = lax.rem(blob, sz.blobs)
        param = spread_rows(param_ref[pl.ds(tile, 1), :], eight)
        pick = lambda k: take(param, jnp.full(eight, k, jnp.int32))
        row_rate = take(param, comp)
        row_amp = take(param, comp + COMPS)
        row_base = pick(2 * COMPS) + spread_rows(row_ref[pl.ds(blob, 1), :], eight)
        col_base = pick(2 * COMPS + 1)
        rate = [pick(g) for g in range(COMPS)]
        col_table = col_ref[zone]
        square = []
        for half in range(2):
            place = take(col_table, jnp.full(eight, half * sz.blobs, jnp.int32) + local)
            away = lane_f - col_base - place
            square.append(away * away)
        cols = [[jnp.exp2(rate[g] * square[half]) for half in range(2)] for g in range(COMPS)]
        heads, tails, heads_f, tails_f = [], [], [], []
        for g in range(COMPS):
            both = jnp.concatenate(cols[g], axis=0)
            head = both.astype(jnp.bfloat16)
            head_f = head.astype(jnp.float32)
            heads.append(head)
            heads_f.append(head_f)
            tails_f.append(both - head_f)
            tails.append(tails_f[-1].astype(jnp.bfloat16))
        rights = []
        for half in range(2):
            span = slice(half * HALF, (half + 1) * HALF)
            top = [h[span] for h in heads_f]
            rights.append(
                jnp.concatenate(top + top + [t[span] for t in tails_f] + [blank], axis=0).astype(
                    jnp.bfloat16
                )
            )
        rows = []
        for part in range(height // 8):
            away = (sub_f + 8.0 * part) - row_base
            value = jnp.exp2(row_rate * (away * away)) * row_amp
            rows.append(value)
            line_ref[slot, 0, part * 8 : (part + 1) * 8, :] = value
            for half in range(2):
                seen = take(value, half_index + half * HALF)
                head = seen.astype(jnp.bfloat16).astype(jnp.float32)
                line_ref[slot, 1 + half, part * 8 : (part + 1) * 8, :] = jnp.where(
                    high_part, head, seen - head
                )
        models = []
        for half in range(2):
            left = []
            for i in range(0, height, 2):
                pair = jnp.concatenate(
                    [
                        spread_rows(line_ref[slot, 1 + half, i + d : i + d + 1, :], eight)
                        for d in range(2)
                    ],
                    axis=0,
                )
                left.append(pair.astype(jnp.bfloat16) * keep)
            models.append(
                lax.dot_general(
                    jnp.concatenate(left, axis=0), rights[half], (((1,), (0,)), ((), ())),
                    preferred_element_type=jnp.float32,
                )
            )
        left = []
        for i in range(height):
            span = slice(i * HALF, (i + 1) * HALF)
            weight = spread_rows(weight_ref[slot, i : i + 1, :], shape)
            scaled = jnp.concatenate([models[0][span], models[1][span]], axis=0) * weight
            left.append(jnp.concatenate(split(scaled), axis=1))
        left.append(jnp.concatenate(split(weight_ref[slot] * pixel_ref[slot]), axis=1))
        top = jnp.concatenate(heads, axis=0)
        right = jnp.concatenate(
            [
                jnp.concatenate([top, top], axis=1),
                jnp.concatenate([jnp.concatenate(tails, axis=0), zero_tail], axis=1),
                zero_rows,
            ],
            axis=0,
        )
        product = lax.dot_general(
            jnp.concatenate(left, axis=0), right, (((1,), (1,)), ((), ())),
            preferred_element_type=jnp.float32,
        )
        normal = None
        for i in range(height):
            line = spread_rows(line_ref[slot, 0, i : i + 1, :], shape)
            term = product[i * SLOTS : (i + 1) * SLOTS] * line
            normal = term if normal is None else normal + term
        vector = None
        for part in range(height // 8):
            at = height * SLOTS + part * 8
            term = product[at : at + 8] * rows[part]
            vector = term if vector is None else vector + term
        folded = jnp.concatenate([normal, vector], axis=0)
        folded = folded + pltpu.roll(folded, LANES - slots_all, 1)
        folded = (
            folded
            + pltpu.roll(folded, LANES - SLOTS, 1)
            + pltpu.roll(folded, LANES - 2 * SLOTS, 1)
        )
        upper, lower, vector = folded[:HALF], folded[HALF:SLOTS], folded[SLOTS:]
        main = jnp.where(
            seat_a, take(upper, index_a), jnp.where(seat_b, take(lower, index_b), 0.0)
        )
        code = (
            lax.div(local, sz.share) * sz.systems
            + band_ref[tile] * sz.share
            + lax.rem(local, sz.share)
        )
        rest = jnp.where(lane == sub, take(upper, sub + HALF), 0.0)
        rest = jnp.where((lane >= SLOTS) & (lane < 2 * SLOTS), pltpu.roll(vector, SLOTS, 1), rest)
        rest = jnp.where((lane == HALF) & (sub == 0), code.astype(jnp.float32), rest)
        order = used_ref[zone]
        used_ref[zone] = order + 1
        out_ref[zone, pl.ds(order, 1), :] = jnp.sum(main, axis=0, keepdims=True)
        rest_ref[zone, pl.ds(order, 1), :] = jnp.sum(rest, axis=0, keepdims=True)

    @pl.when(step == pl.num_programs(0) - 1)
    def _():
        def body(zone, carry):
            total = rest_ref[zone, 0 : sz.rest, :]
            for seat in range(1, SEATS):
                piece = rest_ref[zone, seat * sz.rest : (seat + 1) * sz.rest, :]
                total = total + pltpu.roll(piece, seat * SEAT, 1)
            out_ref[zone, sz.capacity : sz.capacity + sz.rest, :] = total
            return carry

        lax.fori_loop(0, sz.zones, body, 0)


def tile_terms(sz, blob, band, shift, amp, sigma, catalogs, pixels, weights):
    tiles, height, width = pixels.shape
    per = TILES_STEP
    while tiles % per:
        per -= 1
    block = pl.BlockSpec((per, height, width), lambda s: (s, 0, 0))
    turned = -(-sz.zones * HALF // LANES)
    return pl.pallas_call(
        functools.partial(tile_kernel, sz),
        grid=(tiles // per,),
        out_shape=jax.ShapeDtypeStruct((sz.zones, sz.rows, LANES), jnp.float32),
        in_specs=[SMEM] * 2 + [VMEM] * 4 + [block, block],
        out_specs=pl.BlockSpec((sz.zones, sz.rows, LANES), lambda s: (0, 0, 0)),
        scratch_shapes=[
            pltpu.VMEM((turned * LANES, LANES), jnp.float32),
            pltpu.VMEM((turned, LANES, LANES), jnp.float32),
            pltpu.VMEM((sz.zones, HALF, LANES), jnp.float32),
            pltpu.VMEM((sz.zones * sz.blobs, LANES), jnp.float32),
            pltpu.VMEM((tiles, LANES), jnp.float32),
            pltpu.VMEM((per, 3, height, width), jnp.float32),
            pltpu.VMEM((sz.zones, sz.capacity, LANES), jnp.float32),
            pltpu.SMEM((sz.zones,), jnp.int32),
        ],
        compiler_params=pltpu.CompilerParams(dimension_semantics=("arbitrary",)),
    )(blob, band, shift, amp, sigma, catalogs, pixels, weights)


def find_seats(sz, zone, cat_ref, edge_ref, seat_ref):
    shape = (HALF, LANES)
    edges = spread_rows(edge_ref[...], shape)
    source = iota((sz.sources, LANES), 0)
    lane = iota((1, LANES), 1)
    total = None
    for side in range(3):
        near = lax.rem(zone + side - 1 + sz.zones, sz.zones)
        member = cat_ref[near, sz.member_row : sz.member_row + HALF, :].astype(jnp.int32)
        top = sz.edge + sz.sources
        if side == 0:
            valid = (member >= top) & (zone > 0)
            target = take(edges, jnp.where(valid, member - top, 0))
        elif side == 1:
            valid = (member >= sz.edge) & (member < top)
            target = member - sz.edge
        else:
            valid = (member >= 0) & (member < sz.edge) & (zone < sz.zones - 1)
            target = take(edges, jnp.where(valid, member + sz.edge, 0))
        target = jnp.where(valid, target, -1)
        for row in range(HALF):
            hit = source == target[row : row + 1, :]
            right = jnp.where(hit, 1.0, 0.0).astype(jnp.bfloat16)
            slot = side * SLOTS + row + lane // sz.blobs * HALF
            left = jnp.concatenate(
                [slot, lane % sz.blobs, jnp.zeros((SLOTS - 2, LANES), jnp.int32)], axis=0
            )
            part = lax.dot_general(
                left.astype(jnp.float32).astype(jnp.bfloat16), right, (((1,), (1,)), ((), ())),
                preferred_element_type=jnp.float32,
            )
            total = part if total is None else total + part
    seat_ref[...] = total[:8].astype(jnp.int32)


def gather_terms(sz, got_ref, table_ref, part_ref):
    for zone in range(sz.zones):
        start = zone * sz.capacity
        table_ref[start : start + sz.capacity, :LANES] = got_ref[zone, : sz.capacity, :]
        rest = got_ref[zone, sz.capacity : sz.capacity + sz.rest, :]
        for seat in range(SEATS):
            at = start + seat * sz.rest
            table_ref[at : at + sz.rest, LANES:] = (
                pltpu.roll(rest, LANES - seat * SEAT, 1) if seat else rest
            )
    square = (LANES, LANES)
    diagonal = iota(square, 0) == iota(square, 1)
    codes = []
    for at in range(0, sz.entries, LANES):
        block = table_ref[at : at + LANES, LANES:]
        code = take(block, jnp.full(square, HALF, jnp.int32))
        codes.append(jnp.sum(jnp.where(diagonal, code, 0.0), axis=0, keepdims=True))
    codes = jnp.concatenate(codes, axis=1)
    count = sz.bands * sz.block
    system = iota((count, sz.entries), 0)
    hit = jnp.where(system.astype(jnp.float32) == codes, 1.0, 0.0).astype(jnp.bfloat16)
    head, tail = split(table_ref[...])
    dims = (((1,), (0,)), ((), ()))
    total = lax.dot_general(hit, head, dims, preferred_element_type=jnp.float32)
    total = total + lax.dot_general(hit, tail, dims, preferred_element_type=jnp.float32)
    lane = iota((sz.third, LANES), 1) // SEAT
    for owner in range(sz.bands):
        start = owner * sz.block
        part_ref[owner, : sz.block, :] = total[start : start + sz.block, :LANES]
        rest = None
        for seat in range(FILTER_BANDS):
            at = start + seat * sz.third
            piece = total[at : at + sz.third, LANES:]
            piece = jnp.where(lane == seat, pltpu.roll(piece, seat * SEAT, 1) if seat else piece, 0.0)
            rest = piece if rest is None else rest + piece
        part_ref[owner, sz.block :, :] = rest


def solve(sz, summed, flat_ref, square_ref):
    main, rest = summed[: sz.block], summed[sz.block :]
    rest = jnp.concatenate(
        [pltpu.roll(rest, LANES - s * SEAT, 1) if s else rest for s in range(FILTER_BANDS)], axis=0
    )
    fill = jnp.zeros((LANES - sz.block, LANES), jnp.float32)
    flat_ref[:LANES, :] = jnp.concatenate([main, fill], axis=0).T
    flat_ref[LANES:, :] = jnp.concatenate([rest, fill], axis=0).T[: 2 * SLOTS]
    for l in range(SLOTS):
        for j in range(SLOTS):
            away = (l - j) % SLOTS
            if away < HALF:
                at = HALF * j + away
            elif away == HALF:
                at = LANES + min(j, l)
            else:
                at = HALF * l + SLOTS - away
            square_ref[l, j : j + 1, :] = flat_ref[at : at + 1, :]
    shape = (SLOTS, LANES)
    sub = iota(shape, 0)
    columns = [square_ref[l] + jnp.where(sub == l, PRIOR, 0.0) for l in range(SLOTS)]
    columns.append(flat_ref[LANES + SLOTS : LANES + 2 * SLOTS, :])
    scale = columns[0]
    for k in range(SLOTS):
        column = columns[k]
        inverse = 1.0 / column[k : k + 1]
        scale = jnp.where(sub == k, column, scale)
        column = jnp.where(sub == k, 0.0, column)
        for l in range(k + 1, SLOTS + 1):
            ratio = columns[l][k : k + 1] * inverse
            columns[l] = columns[l] - column * ratio
    return columns[SLOTS] / scale


def finish_kernel(
    sz, terms_ref, cat_ref, edge_ref, out_ref,
    got_ref, table_ref, part_ref, sum_ref, flat_ref, square_ref, solved_ref, flux_ref, seat_ref,
    send_term, recv_term, own_term, send_sum, recv_sum, send_flux, recv_flux,
):
    zones, bands = sz.zones, sz.bands
    zone = lax.axis_index("zone")
    band = lax.axis_index("band")
    at = lambda dz, db: (lax.rem(zone + dz, zones), lax.rem(band + db, bands))
    far = [(dz, 0) for dz in range(1, zones)]
    near = [(0, db) for db in range(1, bands)]
    sides = near + [(dz, db) for dz in (1, zones - 1) for db in range(bands)]
    greeted = far + [move for move in sides if move not in far]
    barrier = pltpu.get_barrier_semaphore()
    for move in greeted:
        pl.semaphore_signal(barrier, inc=1, device_id=at(*move), device_id_type=MESH)
    own = pltpu.make_async_copy(terms_ref.at[zone], got_ref.at[zone], own_term)
    own.start()
    pl.semaphore_wait(barrier, len(greeted))
    copies = []
    for order, move in enumerate(far):
        target = at(*move)
        copy = pltpu.make_async_remote_copy(
            src_ref=terms_ref.at[target[0]],
            dst_ref=got_ref.at[zone],
            send_sem=send_term.at[order],
            recv_sem=recv_term.at[order],
            device_id=target,
            device_id_type=MESH,
        )
        copy.start()
        copies.append(copy)
    find_seats(sz, zone, cat_ref, edge_ref, seat_ref)
    own.wait()
    for copy in copies:
        copy.wait()

    gather_terms(sz, got_ref, table_ref, part_ref)
    copies = []
    for order, move in enumerate(near):
        target = at(*move)
        copy = pltpu.make_async_remote_copy(
            src_ref=part_ref.at[target[1]],
            dst_ref=sum_ref.at[order],
            send_sem=send_sum.at[order],
            recv_sem=recv_sum.at[order],
            device_id=target,
            device_id_type=MESH,
        )
        copy.start()
        copies.append(copy)
    for copy in copies:
        copy.wait()
    summed = part_ref[band]
    for order in range(len(near)):
        summed = summed + sum_ref[order]
    solved = solve(sz, summed, flat_ref, square_ref)
    eight = (HALF, LANES)
    packed = jnp.where(
        iota(eight, 1) < LANES // 2, solved[:HALF], pltpu.roll(solved[HALF:], LANES // 2, 1)
    )
    solved_ref[...] = packed
    flux_ref[bands + band] = packed
    copies = []
    for order, move in enumerate(sides):
        side = {0: 1, 1: 0, zones - 1: 2}[move[0]]
        copy = pltpu.make_async_remote_copy(
            src_ref=solved_ref,
            dst_ref=flux_ref.at[side * bands + band],
            send_sem=send_flux.at[order],
            recv_sem=recv_flux.at[order],
            device_id=at(*move),
            device_id_type=MESH,
        )
        copy.start()
        copies.append(copy)
    for copy in copies:
        copy.wait()

    sub = iota(eight, 0)
    for part in range(sz.parts):
        span = slice(part * LANES, (part + 1) * LANES)
        slot = spread_rows(seat_ref[0:1, span], eight)
        blob = spread_rows(seat_ref[1:2, span], eight)
        row = slot % SLOTS
        key = slot // SLOTS * bands + blob // sz.share
        index = row // HALF * (LANES // 2) + blob % sz.share
        key = jnp.where(sub == row % HALF, key, -1)
        values = [jnp.zeros(eight, jnp.float32) for _ in range(FILTER_BANDS)]
        for table in range(3 * bands):
            flux = flux_ref[table]
            hit = key == table
            for k in range(FILTER_BANDS):
                values[k] = jnp.where(hit, take(flux, index + k * sz.share), values[k])
        out_ref[:, span] = jnp.concatenate(
            [jnp.sum(value, axis=0, keepdims=True) for value in values], axis=0
        )


def on_device(
    sizes, pixels, inv_var, tile_offset, psf_amp, psf_sigma, tile_blob, tile_band,
    source_pos, edge_rows, blob_members, sources_per_blob,
):
    zones, bands = sizes
    sz = Sizes(
        zones, bands, source_pos.shape[1], edge_rows.shape[0] // 2,
        sources_per_blob.shape[0], pixels.shape[0],
    )
    edges = edge_rows.reshape(1, -1)
    dma = pltpu.SemaphoreType.DMA
    catalogs = pl.pallas_call(
        functools.partial(catalog_kernel, sz),
        out_shape=jax.ShapeDtypeStruct((zones, sz.cat_rows, LANES), jnp.float32),
        in_specs=[VMEM] * 4,
        out_specs=VMEM,
        scratch_shapes=[
            pltpu.VMEM((sz.cat_rows, LANES), jnp.float32),
            dma((zones - 1,)), dma((zones - 1,)), dma,
        ],
        compiler_params=pltpu.CompilerParams(collective_id=0, has_side_effects=True),
    )(source_pos, edges, blob_members.T, sources_per_blob.reshape(1, -1))
    terms = tile_terms(
        sz, tile_blob, tile_band, tile_offset, psf_amp, psf_sigma, catalogs, pixels, inv_var
    )
    near = 3 * bands - 1
    rows = sz.block + sz.third
    return pl.pallas_call(
        functools.partial(finish_kernel, sz),
        out_shape=jax.ShapeDtypeStruct((FILTER_BANDS, sz.sources), jnp.float32),
        in_specs=[ANY, VMEM, VMEM],
        out_specs=VMEM,
        scratch_shapes=[
            pltpu.VMEM((zones, sz.rows, LANES), jnp.float32),
            pltpu.VMEM((sz.entries, 2 * LANES), jnp.float32),
            pltpu.VMEM((bands, rows, LANES), jnp.float32),
            pltpu.VMEM((bands - 1, rows, LANES), jnp.float32),
            pltpu.VMEM((LANES + 2 * SLOTS, LANES), jnp.float32),
            pltpu.VMEM((SLOTS, SLOTS, LANES), jnp.float32),
            pltpu.VMEM((HALF, LANES), jnp.float32),
            pltpu.VMEM((3 * bands, HALF, LANES), jnp.float32),
            pltpu.VMEM((8, sz.sources), jnp.int32),
            dma((zones - 1,)), dma((zones - 1,)), dma,
            dma((bands - 1,)), dma((bands - 1,)),
            dma((near,)), dma((near,)),
        ],
        compiler_params=pltpu.CompilerParams(collective_id=1, has_side_effects=True),
    )(terms, catalogs, edges)


def solution(mesh):
    sizes = (mesh.shape["zone"], mesh.shape["band"])
    return jax.shard_map(
        functools.partial(on_device, sizes),
        mesh=mesh,
        in_specs=(
            P(("zone", "band"), None, None),
            P(("zone", "band"), None, None),
            P(None, ("zone", "band")),
            P(None, ("zone", "band")),
            P(None, ("zone", "band")),
            P(("zone", "band")),
            P(("zone", "band")),
            P(None, "zone"),
            P("zone"),
            P("zone", None),
            P("zone"),
        ),
        out_specs=P(None, "zone"),
        check_vma=False,
    )
```

```python
import functools
import math

import jax
import jax.numpy as jnp
from jax import lax
from jax.experimental import pallas as pl
from jax.experimental.pallas import tpu as pltpu
from jax.sharding import PartitionSpec as P

FILTER_BANDS = 3
COMPS = 3
SLOTS = 16
HALF = SLOTS // 2
LANES = 128
SEATS = 4
SEAT = LANES // SEATS
TILES_STEP = 32
PRIOR = 1.0
FAR = 1.0e4
LOG2E = math.log2(math.e)

VMEM = pl.BlockSpec(memory_space=pltpu.VMEM)
SMEM = pl.BlockSpec(memory_space=pltpu.SMEM)
ANY = pl.BlockSpec(memory_space=pl.ANY)
MESH = pl.DeviceIdType.MESH


def iota(shape, axis):
    return lax.broadcasted_iota(jnp.int32, shape, axis)


def take(table, index):
    return jnp.take_along_axis(table, index, axis=1, mode="promise_in_bounds")


def spread_rows(row, shape):
    return jnp.broadcast_to(row, shape)


def lookup(rows, index):
    found = jnp.zeros(index.shape, rows[0].dtype)
    low = index & (LANES - 1)
    for part, row in enumerate(rows):
        hit = take(spread_rows(row, index.shape), low)
        found = jnp.where(index // LANES == part, hit, found)
    return found


def partner(zone, step, zones):
    if zones & (zones - 1):
        return lax.rem(zone + step, zones)
    other = 0
    bit = 1
    while bit < zones:
        digit = lax.rem(lax.div(zone, bit), 2)
        other = other + bit * ((1 - digit) if step & bit else digit)
        bit *= 2
    return other


class Sizes:
    def __init__(self, zones, bands, sources, edge, blobs, tiles):
        self.zones, self.bands = zones, bands
        self.sources, self.edge, self.blobs, self.tiles = sources, edge, blobs, tiles
        self.parts = sources // LANES
        self.member_row = -(-2 * self.parts // 8) * 8
        self.edge_row = self.member_row + HALF
        self.cat_rows = self.edge_row + 8
        self.sent_rows = self.edge_row + 2
        capacity = max(SEATS, (2 * tiles + zones - 1) // zones)
        self.capacity = -(-capacity // SEATS) * SEATS
        self.rest = self.capacity // SEATS
        self.rows = -(-(self.capacity + self.rest) // 8) * 8
        self.share = blobs // bands
        self.systems = FILTER_BANDS * self.share
        self.block = -(-self.systems // 8) * 8
        self.third = self.block // FILTER_BANDS
        self.entries = zones * self.capacity


def catalog_kernel(
    sz, source_ref, edge_ref, member_ref, count_ref, sigma_ref, out_ref, rate_ref,
    pack_ref, send_sem, recv_sem, own_sem,
):
    zones = sz.zones
    zone = lax.axis_index("zone")
    band = lax.axis_index("band")
    barrier = pltpu.get_barrier_semaphore()
    targets = [(partner(zone, step, zones), band) for step in range(zones - 1, 0, -1)]
    for target in targets:
        pl.semaphore_signal(barrier, inc=1, device_id=target, device_id_type=MESH)
    shape = (8, LANES)
    edges = spread_rows(edge_ref[...], shape)
    for coord in range(2):
        rows = []
        for part in range(sz.parts):
            row = source_ref[coord : coord + 1, part * LANES : (part + 1) * LANES]
            pack_ref[coord * sz.parts + part : coord * sz.parts + part + 1, :] = row
            rows.append(row)
        at = sz.edge_row + coord
        pack_ref[at : at + 1, :] = lookup(rows, edges)[:1]
    slot = iota((SLOTS, sz.blobs), 0)
    member = jnp.where(slot < count_ref[...], member_ref[...], -1).astype(jnp.float32)
    pack_ref[sz.member_row : sz.member_row + HALF, :] = jnp.concatenate(
        [member[:HALF], member[HALF:]], axis=1
    )
    sent = pl.ds(0, sz.sent_rows)
    own = pltpu.make_async_copy(pack_ref.at[sent], out_ref.at[zone, sent], own_sem)
    own.start()
    pl.semaphore_wait(barrier, len(targets))
    copies = []
    for order, target in enumerate(targets):
        copy = pltpu.make_async_remote_copy(
            src_ref=pack_ref.at[sent],
            dst_ref=out_ref.at[zone, sent],
            send_sem=send_sem.at[order],
            recv_sem=recv_sem.at[order],
            device_id=target,
            device_id_type=MESH,
        )
        copy.start()
        copies.append(copy)
    sigma = sigma_ref[...]
    rate_ref[...] = (-0.5 * LOG2E) / (sigma * sigma)
    own.wait()
    for copy in copies:
        copy.wait()


def resolve_zone(sz, zone, cat_ref, stage_ref, col_ref):
    shape = (HALF, LANES)
    member = cat_ref[zone, sz.member_row : sz.member_row + HALF, :].astype(jnp.int32)
    if isinstance(zone, int):
        before, after = max(zone - 1, 0), min(zone + 1, sz.zones - 1)
    else:
        before, after = jnp.maximum(zone - 1, 0), jnp.minimum(zone + 1, sz.zones - 1)
    low = member < sz.edge
    high = member >= sz.edge + sz.sources
    own = jnp.clip(member - sz.edge, 0, sz.sources - 1)
    rim = jnp.where(
        low, sz.edge + jnp.maximum(member, 0), jnp.where(high, member - sz.edge - sz.sources, 0)
    )
    lane = iota(shape, 1)
    for coord in range(2):
        rows = [
            cat_ref[zone, coord * sz.parts + part : coord * sz.parts + part + 1, :]
            for part in range(sz.parts)
        ]
        at = sz.edge_row + coord
        table = jnp.where(
            lane >= sz.edge,
            spread_rows(cat_ref[before, at : at + 1, :], shape),
            spread_rows(cat_ref[after, at : at + 1, :], shape),
        )
        place = jnp.where(low | high, take(table, rim), lookup(rows, own))
        if coord == 0:
            place = jnp.where(member < 0, FAR, place)
            start = zone * HALF if isinstance(zone, int) else pl.multiple_of(zone * HALF, HALF)
            stage_ref[pl.ds(start, HALF), :] = place
        else:
            col_ref[zone] = place


def spread_zone(sz, zone, turned_ref, row_ref):
    shape = (8, LANES)
    lane = iota(shape, 1)
    per = LANES // HALF
    index = (zone % per) * HALF + lane % HALF
    upper = lane % SLOTS >= HALF
    for part in range(sz.blobs // 8):
        pieces = []
        for half in range(2):
            at = half * sz.blobs + part * 8
            pieces.append(take(turned_ref[zone // per, at : at + 8, :], index))
        start = zone * sz.blobs + part * 8
        if not isinstance(zone, int):
            start = pl.multiple_of(start, 8)
        row_ref[pl.ds(start, 8), :] = jnp.where(upper, pieces[1], pieces[0])


def prepare(sz, cat_ref, stage_ref, turned_ref, col_ref, row_ref):
    each = (lambda body: [body(z) for z in range(sz.zones)]) if sz.zones <= 8 else (
        lambda body: lax.fori_loop(0, sz.zones, lambda z, c: (body(z), c)[1], 0)
    )
    each(lambda z: resolve_zone(sz, z, cat_ref, stage_ref, col_ref))
    for part in range(turned_ref.shape[0]):
        turned_ref[part] = stage_ref[part * LANES : (part + 1) * LANES, :].T
    each(lambda z: spread_zone(sz, z, turned_ref, row_ref))


def split(value):
    head = value.astype(jnp.bfloat16)
    return head, (value - head.astype(jnp.float32)).astype(jnp.bfloat16)


def tile_kernel(
    sz, blob_ref, band_ref, shift_ref, amp_ref, rate_ref, cat_ref, pixel_ref, weight_ref,
    out_ref, stage_ref, turned_ref, col_ref, row_ref, line_ref, rest_ref, used_ref,
):
    step = pl.program_id(0)
    per, height, _ = pixel_ref.shape

    @pl.when(step == 0)
    def _():
        out_ref[...] = jnp.zeros_like(out_ref)
        rest_ref[...] = jnp.zeros_like(rest_ref)
        for zone in range(sz.zones):
            used_ref[zone] = 0
        prepare(sz, cat_ref, stage_ref, turned_ref, col_ref, row_ref)

    eight = (HALF, LANES)
    shape = (SLOTS, LANES)
    lane = iota(eight, 1)
    sub = iota(eight, 0)
    sub_f = sub.astype(jnp.float32)
    lane_f = lane.astype(jnp.float32)
    slots_all = COMPS * SLOTS
    width = COMPS * HALF
    keep = (iota(shape, 1) % HALF == iota(shape, 0) % HALF) & (iota(shape, 1) < 3 * width)
    keep = jnp.where(keep, 1.0, 0.0).astype(jnp.bfloat16)
    comp = lane // SLOTS % COMPS
    high_part = (lane < width) | (lane >= 2 * width)
    half_index = lane // HALF % COMPS * SLOTS + lane % HALF
    seat_a = lane // HALF == sub
    seat_b = lane // HALF == sub + HALF
    blank = jnp.zeros((LANES - 3 * width, LANES), jnp.float32)
    zero_tail = jnp.zeros((slots_all, LANES), jnp.bfloat16)
    zero_rows = jnp.zeros((LANES - 2 * slots_all, 2 * LANES), jnp.bfloat16)

    for slot in range(per):
        tile = step * per + slot
        blob = blob_ref[tile]
        zone = lax.div(blob, sz.blobs)
        local = lax.rem(blob, sz.blobs)
        rate = [rate_ref[g, tile] for g in range(COMPS)]
        amp = [amp_ref[g, tile] for g in range(COMPS)]
        row_rate = jnp.where(comp == 0, rate[0], jnp.where(comp == 1, rate[1], rate[2]))
        row_amp = jnp.where(comp == 0, amp[0], jnp.where(comp == 1, amp[1], amp[2]))
        row_shift = shift_ref[0, tile]
        row_base = row_shift + spread_rows(row_ref[pl.ds(blob, 1), :], eight)
        col_base = shift_ref[1, tile]
        col_table = col_ref[zone]
        square = []
        for half in range(2):
            index = jnp.full(eight, half * sz.blobs, jnp.int32) + local
            away = lane_f - col_base - take(col_table, index)
            square.append(away * away)
        cols = [[jnp.exp2(rate[g] * square[half]) for half in range(2)] for g in range(COMPS)]
        heads, tails, heads_f, tails_f = [], [], [], []
        for g in range(COMPS):
            both = jnp.concatenate(cols[g], axis=0)
            head = both.astype(jnp.bfloat16)
            head_f = head.astype(jnp.float32)
            heads.append(head)
            heads_f.append(head_f)
            tails_f.append(both - head_f)
            tails.append(tails_f[-1].astype(jnp.bfloat16))
        rights = []
        for half in range(2):
            span = slice(half * HALF, (half + 1) * HALF)
            top = [h[span] for h in heads_f]
            rights.append(
                jnp.concatenate(top + top + [t[span] for t in tails_f] + [blank], axis=0).astype(
                    jnp.bfloat16
                )
            )
        rows = []
        for part in range(height // 8):
            away = (sub_f + 8.0 * part) - row_base
            value = jnp.exp2(row_rate * (away * away)) * row_amp
            rows.append(value)
            line_ref[slot, 0, part * 8 : (part + 1) * 8, :] = value
            for half in range(2):
                seen = take(value, half_index + half * HALF)
                head = seen.astype(jnp.bfloat16).astype(jnp.float32)
                line_ref[slot, 1 + half, part * 8 : (part + 1) * 8, :] = jnp.where(
                    high_part, head, seen - head
                )
        models = []
        for half in range(2):
            left = []
            for i in range(0, height, 2):
                pair = jnp.concatenate(
                    [
                        spread_rows(line_ref[slot, 1 + half, i + d : i + d + 1, :], eight)
                        for d in range(2)
                    ],
                    axis=0,
                )
                left.append(pair.astype(jnp.bfloat16) * keep)
            models.append(
                lax.dot_general(
                    jnp.concatenate(left, axis=0), rights[half], (((1,), (0,)), ((), ())),
                    preferred_element_type=jnp.float32,
                )
            )
        left = []
        for i in range(height):
            span = slice(i * HALF, (i + 1) * HALF)
            weight = spread_rows(weight_ref[slot, i : i + 1, :], shape)
            scaled = jnp.concatenate([models[0][span], models[1][span]], axis=0) * weight
            left.append(jnp.concatenate(split(scaled), axis=1))
        left.append(jnp.concatenate(split(weight_ref[slot] * pixel_ref[slot]), axis=1))
        top = jnp.concatenate(heads, axis=0)
        right = jnp.concatenate(
            [
                jnp.concatenate([top, top], axis=1),
                jnp.concatenate([jnp.concatenate(tails, axis=0), zero_tail], axis=1),
                zero_rows,
            ],
            axis=0,
        )
        product = lax.dot_general(
            jnp.concatenate(left, axis=0), right, (((1,), (1,)), ((), ())),
            preferred_element_type=jnp.float32,
        )
        normal = None
        for i in range(height):
            line = spread_rows(line_ref[slot, 0, i : i + 1, :], shape)
            term = product[i * SLOTS : (i + 1) * SLOTS] * line
            normal = term if normal is None else normal + term
        vector = None
        for part in range(height // 8):
            at = height * SLOTS + part * 8
            term = product[at : at + 8] * rows[part]
            vector = term if vector is None else vector + term
        folded = jnp.concatenate([normal, vector], axis=0)
        for shift in (LANES // 2, LANES // 4, LANES // 8):
            folded = folded + pltpu.roll(folded, shift, 1)
        upper, lower, vector = folded[:HALF], folded[HALF:SLOTS], folded[SLOTS:]
        step_back = SLOTS - HALF - 1
        main = jnp.where(
            seat_a, pltpu.roll(upper, 0, 1, stride=step_back, stride_axis=0),
            jnp.where(
                seat_b,
                pltpu.roll(lower, HALF * step_back, 1, stride=step_back, stride_axis=0), 0.0,
            ),
        )
        code = (
            lax.div(local, sz.share) * sz.systems
            + band_ref[tile] * sz.share
            + lax.rem(local, sz.share)
        )
        rest = jnp.where(lane == sub, pltpu.roll(upper, HALF, 1), 0.0)
        rest = jnp.where((lane >= SLOTS) & (lane < 2 * SLOTS), vector, rest)
        rest = jnp.where((lane == HALF) & (sub == 0), code.astype(jnp.float32), rest)
        order = used_ref[zone]
        used_ref[zone] = order + 1
        out_ref[zone, pl.ds(order, 1), :] = jnp.sum(main, axis=0, keepdims=True)
        rest_ref[zone, pl.ds(order, 1), :] = jnp.sum(rest, axis=0, keepdims=True)

    @pl.when(step == pl.num_programs(0) - 1)
    def _():
        def body(zone, carry):
            total = rest_ref[zone, 0 : sz.rest, :]
            for seat in range(1, SEATS):
                piece = rest_ref[zone, seat * sz.rest : (seat + 1) * sz.rest, :]
                total = total + pltpu.roll(piece, seat * SEAT, 1)
            out_ref[zone, sz.capacity : sz.capacity + sz.rest, :] = total
            return carry

        lax.fori_loop(0, sz.zones, body, 0)


def tile_terms(sz, blob, band, shift, amp, rate, catalogs, pixels, weights):
    tiles, height, width = pixels.shape
    per = TILES_STEP
    while tiles % per:
        per -= 1
    block = pl.BlockSpec((per, height, width), lambda s: (s, 0, 0))
    turned = -(-sz.zones * HALF // LANES)
    return pl.pallas_call(
        functools.partial(tile_kernel, sz),
        grid=(tiles // per,),
        out_shape=jax.ShapeDtypeStruct((sz.zones, sz.rows, LANES), jnp.float32),
        in_specs=[SMEM] * 5 + [VMEM, block, block],
        out_specs=pl.BlockSpec((sz.zones, sz.rows, LANES), lambda s: (0, 0, 0)),
        scratch_shapes=[
            pltpu.VMEM((turned * LANES, LANES), jnp.float32),
            pltpu.VMEM((turned, LANES, LANES), jnp.float32),
            pltpu.VMEM((sz.zones, HALF, LANES), jnp.float32),
            pltpu.VMEM((sz.zones * sz.blobs, LANES), jnp.float32),
            pltpu.VMEM((per, 3, height, width), jnp.float32),
            pltpu.VMEM((sz.zones, sz.capacity, LANES), jnp.float32),
            pltpu.SMEM((sz.zones,), jnp.int32),
        ],
        compiler_params=pltpu.CompilerParams(dimension_semantics=("arbitrary",)),
    )(blob, band, shift, amp, rate, catalogs, pixels, weights)


def find_seats(sz, zone, cat_ref, edge_ref, seat_ref):
    shape = (HALF, LANES)
    edges = spread_rows(edge_ref[...], shape)
    source = iota((sz.sources, LANES), 0)
    lane = iota((1, LANES), 1)
    total = None
    for side in range(3):
        near = lax.rem(zone + side - 1 + sz.zones, sz.zones)
        member = cat_ref[near, sz.member_row : sz.member_row + HALF, :].astype(jnp.int32)
        top = sz.edge + sz.sources
        if side == 0:
            valid = (member >= top) & (zone > 0)
            target = take(edges, jnp.where(valid, member - top, 0))
        elif side == 1:
            valid = (member >= sz.edge) & (member < top)
            target = member - sz.edge
        else:
            valid = (member >= 0) & (member < sz.edge) & (zone < sz.zones - 1)
            target = take(edges, jnp.where(valid, member + sz.edge, 0))
        target = jnp.where(valid, target, -1)
        for row in range(HALF):
            hit = source == target[row : row + 1, :]
            right = jnp.where(hit, 1.0, 0.0).astype(jnp.bfloat16)
            slot = side * SLOTS + row + lane // sz.blobs * HALF
            left = jnp.concatenate(
                [slot, lane % sz.blobs, jnp.zeros((SLOTS - 2, LANES), jnp.int32)], axis=0
            )
            part = lax.dot_general(
                left.astype(jnp.float32).astype(jnp.bfloat16), right, (((1,), (1,)), ((), ())),
                preferred_element_type=jnp.float32,
            )
            total = part if total is None else total + part
    seat_ref[...] = total[:8].astype(jnp.int32)


def gather_terms(sz, got_ref, table_ref, part_ref):
    for zone in range(sz.zones):
        start = zone * sz.capacity
        table_ref[start : start + sz.capacity, :LANES] = got_ref[zone, : sz.capacity, :]
        rest = got_ref[zone, sz.capacity : sz.capacity + sz.rest, :]
        for seat in range(SEATS):
            at = start + seat * sz.rest
            table_ref[at : at + sz.rest, LANES:] = (
                pltpu.roll(rest, LANES - seat * SEAT, 1) if seat else rest
            )
    square = (LANES, LANES)
    diagonal = iota(square, 0) == iota(square, 1)
    codes = []
    for at in range(0, sz.entries, LANES):
        block = table_ref[at : at + LANES, LANES:]
        code = take(block, jnp.full(square, HALF, jnp.int32))
        codes.append(jnp.sum(jnp.where(diagonal, code, 0.0), axis=0, keepdims=True))
    codes = jnp.concatenate(codes, axis=1)
    count = sz.bands * sz.block
    system = iota((count, sz.entries), 0)
    hit = jnp.where(system.astype(jnp.float32) == codes, 1.0, 0.0).astype(jnp.bfloat16)
    head, tail = split(table_ref[...])
    dims = (((1,), (0,)), ((), ()))
    total = lax.dot_general(hit, head, dims, preferred_element_type=jnp.float32)
    total = total + lax.dot_general(hit, tail, dims, preferred_element_type=jnp.float32)
    lane = iota((sz.third, LANES), 1) // SEAT
    for owner in range(sz.bands):
        start = owner * sz.block
        part_ref[owner, : sz.block, :] = total[start : start + sz.block, :LANES]
        rest = None
        for seat in range(FILTER_BANDS):
            at = start + seat * sz.third
            piece = total[at : at + sz.third, LANES:]
            piece = jnp.where(lane == seat, pltpu.roll(piece, seat * SEAT, 1) if seat else piece, 0.0)
            rest = piece if rest is None else rest + piece
        part_ref[owner, sz.block :, :] = rest


def solve(sz, summed, flat_ref, square_ref):
    main, rest = summed[: sz.block], summed[sz.block :]
    rest = jnp.concatenate(
        [pltpu.roll(rest, LANES - s * SEAT, 1) if s else rest for s in range(FILTER_BANDS)], axis=0
    )
    fill = jnp.zeros((LANES - sz.block, LANES), jnp.float32)
    flat_ref[:LANES, :] = jnp.concatenate([main, fill], axis=0).T
    flat_ref[LANES:, :] = jnp.concatenate([rest, fill], axis=0).T[: 2 * SLOTS]
    for l in range(SLOTS):
        for j in range(SLOTS):
            away = (l - j) % SLOTS
            if away < HALF:
                at = HALF * j + away
            elif away == HALF:
                at = LANES + min(j, l)
            else:
                at = HALF * l + SLOTS - away
            square_ref[l, j : j + 1, :] = flat_ref[at : at + 1, :]
    shape = (SLOTS, LANES)
    sub = iota(shape, 0)
    columns = [square_ref[l] + jnp.where(sub == l, PRIOR, 0.0) for l in range(SLOTS)]
    columns.append(flat_ref[LANES + SLOTS : LANES + 2 * SLOTS, :])
    scale = columns[0]
    for k in range(SLOTS):
        column = columns[k]
        inverse = 1.0 / column[k : k + 1]
        scale = jnp.where(sub == k, column, scale)
        column = jnp.where(sub == k, 0.0, column)
        for l in range(k + 1, SLOTS + 1):
            ratio = columns[l][k : k + 1] * inverse
            columns[l] = columns[l] - column * ratio
    return columns[SLOTS] / scale


def finish_kernel(
    sz, terms_ref, cat_ref, edge_ref, out_ref,
    got_ref, table_ref, part_ref, sum_ref, flat_ref, square_ref, solved_ref, flux_ref, seat_ref,
    send_term, recv_term, own_term, send_sum, recv_sum, send_flux, recv_flux,
):
    zones, bands = sz.zones, sz.bands
    zone = lax.axis_index("zone")
    band = lax.axis_index("band")
    at = lambda dz, db: (lax.rem(zone + dz + zones, zones), lax.rem(band + db, bands))
    far = [(partner(zone, step, zones), band) for step in range(zones - 1, 0, -1)]
    near = [at(0, db) for db in range(1, bands)]
    above, below = zone < zones - 1, zone > 0
    beside = [(1, above, below), (-1, below, above)]
    barrier = pltpu.get_barrier_semaphore()

    def greet(target):
        pl.semaphore_signal(barrier, inc=1, device_id=target, device_id_type=MESH)

    for target in far + near:
        greet(target)
    for dz, sends, _ in beside:

        @pl.when(sends)
        def _():
            for db in range(1, bands):
                greet(at(dz, db))

    own = pltpu.make_async_copy(terms_ref.at[zone], got_ref.at[zone], own_term)
    own.start()
    ends = lax.div(zone, zones - 1) + lax.div(zones - 1 - zone, zones - 1)
    pl.semaphore_wait(barrier, len(far) + len(near) + (bands - 1) * (2 - ends))
    copies = []
    for order, target in enumerate(far):
        copy = pltpu.make_async_remote_copy(
            src_ref=terms_ref.at[target[0]],
            dst_ref=got_ref.at[zone],
            send_sem=send_term.at[order],
            recv_sem=recv_term.at[order],
            device_id=target,
            device_id_type=MESH,
        )
        copy.start()
        copies.append(copy)
    find_seats(sz, zone, cat_ref, edge_ref, seat_ref)
    own.wait()
    for copy in copies:
        copy.wait()

    gather_terms(sz, got_ref, table_ref, part_ref)
    copies = []
    for order, target in enumerate(near):
        copy = pltpu.make_async_remote_copy(
            src_ref=part_ref.at[target[1]],
            dst_ref=sum_ref.at[order],
            send_sem=send_sum.at[order],
            recv_sem=recv_sum.at[order],
            device_id=target,
            device_id_type=MESH,
        )
        copy.start()
        copies.append(copy)
    for copy in copies:
        copy.wait()
    summed = part_ref[band]
    for order in range(len(near)):
        summed = summed + sum_ref[order]
    solved = solve(sz, summed, flat_ref, square_ref)
    eight = (HALF, LANES)
    packed = jnp.where(
        iota(eight, 1) < LANES // 2, solved[:HALF], pltpu.roll(solved[HALF:], LANES // 2, 1)
    )
    solved_ref[...] = packed
    flux_ref[bands + band] = packed

    def flux_copy(order, side, target):
        return pltpu.make_async_remote_copy(
            src_ref=solved_ref,
            dst_ref=flux_ref.at[side * bands + band],
            send_sem=send_flux.at[order],
            recv_sem=recv_flux.at[order],
            device_id=target,
            device_id_type=MESH,
        )

    across = []
    for number, (dz, sends, receives) in enumerate(beside):
        first = bands - 1 + number * bands
        group = [flux_copy(first + db, 1 - dz, at(dz, db)) for db in range(bands)]
        across.append((group, sends, receives))

        @pl.when(sends)
        def _():
            for copy in group:
                copy.start()

    copies = [flux_copy(order, 1, target) for order, target in enumerate(near)]
    for copy in copies:
        copy.start()
    for copy in copies:
        copy.wait()
    for group, sends, receives in across:

        @pl.when(sends)
        def _():
            for copy in group:
                copy.wait_send()

        @pl.when(receives)
        def _():
            for copy in group:
                copy.wait_recv()

    sub = iota(eight, 0)
    for part in range(sz.parts):
        span = slice(part * LANES, (part + 1) * LANES)
        slot = spread_rows(seat_ref[0:1, span], eight)
        blob = spread_rows(seat_ref[1:2, span], eight)
        row = slot % SLOTS
        key = slot // SLOTS * bands + blob // sz.share
        index = row // HALF * (LANES // 2) + blob % sz.share
        key = jnp.where(sub == row % HALF, key, -1)
        values = [jnp.zeros(eight, jnp.float32) for _ in range(FILTER_BANDS)]
        for table in range(3 * bands):
            flux = flux_ref[table]
            hit = key == table
            for k in range(FILTER_BANDS):
                values[k] = jnp.where(hit, take(flux, index + k * sz.share), values[k])
        out_ref[:, span] = jnp.concatenate(
            [jnp.sum(value, axis=0, keepdims=True) for value in values], axis=0
        )


def on_device(
    sizes, pixels, inv_var, tile_offset, psf_amp, psf_sigma, tile_blob, tile_band,
    source_pos, edge_rows, blob_members, sources_per_blob,
):
    zones, bands = sizes
    sz = Sizes(
        zones, bands, source_pos.shape[1], edge_rows.shape[0] // 2,
        sources_per_blob.shape[0], pixels.shape[0],
    )
    edges = edge_rows.reshape(1, -1)
    dma = pltpu.SemaphoreType.DMA
    catalogs, rate = pl.pallas_call(
        functools.partial(catalog_kernel, sz),
        out_shape=(
            jax.ShapeDtypeStruct((zones, sz.cat_rows, LANES), jnp.float32),
            jax.ShapeDtypeStruct(psf_sigma.shape, jnp.float32),
        ),
        in_specs=[VMEM] * 5,
        out_specs=(VMEM, VMEM),
        scratch_shapes=[
            pltpu.VMEM((sz.cat_rows, LANES), jnp.float32),
            dma((zones - 1,)), dma((zones - 1,)), dma,
        ],
        compiler_params=pltpu.CompilerParams(collective_id=0, has_side_effects=True),
    )(source_pos, edges, blob_members.T, sources_per_blob.reshape(1, -1), psf_sigma)
    terms = tile_terms(
        sz, tile_blob, tile_band, tile_offset, psf_amp, rate, catalogs, pixels, inv_var
    )
    near = 3 * bands - 1
    rows = sz.block + sz.third
    return pl.pallas_call(
        functools.partial(finish_kernel, sz),
        out_shape=jax.ShapeDtypeStruct((FILTER_BANDS, sz.sources), jnp.float32),
        in_specs=[ANY, VMEM, VMEM],
        out_specs=VMEM,
        scratch_shapes=[
            pltpu.VMEM((zones, sz.rows, LANES), jnp.float32),
            pltpu.VMEM((sz.entries, 2 * LANES), jnp.float32),
            pltpu.VMEM((bands, rows, LANES), jnp.float32),
            pltpu.VMEM((bands - 1, rows, LANES), jnp.float32),
            pltpu.VMEM((LANES + 2 * SLOTS, LANES), jnp.float32),
            pltpu.VMEM((SLOTS, SLOTS, LANES), jnp.float32),
            pltpu.VMEM((HALF, LANES), jnp.float32),
            pltpu.VMEM((3 * bands, HALF, LANES), jnp.float32),
            pltpu.VMEM((8, sz.sources), jnp.int32),
            dma((zones - 1,)), dma((zones - 1,)), dma,
            dma((bands - 1,)), dma((bands - 1,)),
            dma((near,)), dma((near,)),
        ],
        compiler_params=pltpu.CompilerParams(collective_id=1, has_side_effects=True),
    )(terms, catalogs, edges)


def solution(mesh):
    sizes = (mesh.shape["zone"], mesh.shape["band"])
    return jax.shard_map(
        functools.partial(on_device, sizes),
        mesh=mesh,
        in_specs=(
            P(("zone", "band"), None, None),
            P(("zone", "band"), None, None),
            P(None, ("zone", "band")),
            P(None, ("zone", "band")),
            P(None, ("zone", "band")),
            P(("zone", "band")),
            P(("zone", "band")),
            P(None, "zone"),
            P("zone"),
            P("zone", None),
            P("zone"),
        ),
        out_specs=P(None, "zone"),
        check_vma=False,
    )
```

```python
import functools
import math

import jax
import jax.numpy as jnp
from jax import lax
from jax.experimental import pallas as pl
from jax.experimental.pallas import tpu as pltpu
from jax.sharding import PartitionSpec as P

FILTER_BANDS = 3
COMPS = 3
SLOTS = 16
HALF = SLOTS // 2
LANES = 128
SEATS = 4
SEAT = LANES // SEATS
TILES_STEP = 32
PRIOR = 1.0
FAR = 1.0e4
LOG2E = math.log2(math.e)

VMEM = pl.BlockSpec(memory_space=pltpu.VMEM)
SMEM = pl.BlockSpec(memory_space=pltpu.SMEM)
ANY = pl.BlockSpec(memory_space=pl.ANY)
MESH = pl.DeviceIdType.MESH


def iota(shape, axis):
    return lax.broadcasted_iota(jnp.int32, shape, axis)


def take(table, index):
    return jnp.take_along_axis(table, index, axis=1, mode="promise_in_bounds")


def spread_rows(row, shape):
    return jnp.broadcast_to(row, shape)


def lookup(rows, index):
    found = jnp.zeros(index.shape, rows[0].dtype)
    low = index & (LANES - 1)
    for part, row in enumerate(rows):
        hit = take(spread_rows(row, index.shape), low)
        found = jnp.where(index // LANES == part, hit, found)
    return found


def partner(zone, step, zones):
    if zones & (zones - 1):
        return lax.rem(zone + step, zones)
    other = 0
    bit = 1
    while bit < zones:
        digit = lax.rem(lax.div(zone, bit), 2)
        other = other + bit * ((1 - digit) if step & bit else digit)
        bit *= 2
    return other


class Sizes:
    def __init__(self, zones, bands, sources, edge, blobs, tiles):
        self.zones, self.bands = zones, bands
        self.sources, self.edge, self.blobs, self.tiles = sources, edge, blobs, tiles
        self.parts = sources // LANES
        self.member_row = -(-2 * self.parts // 8) * 8
        self.edge_row = self.member_row + HALF
        self.cat_rows = self.edge_row + 8
        self.sent_rows = self.edge_row + 2
        capacity = max(SEATS, (2 * tiles + zones - 1) // zones)
        self.capacity = -(-capacity // SEATS) * SEATS
        self.rest = self.capacity // SEATS
        self.rows = -(-(self.capacity + self.rest) // 8) * 8
        self.share = blobs // bands
        self.systems = FILTER_BANDS * self.share
        self.block = -(-self.systems // 8) * 8
        self.third = self.block // FILTER_BANDS
        self.entries = zones * self.capacity


def pack_catalog(sz, source_ref, edge_ref, member_ref, count_ref, pack_ref):
    shape = (8, LANES)
    edges = spread_rows(edge_ref[...], shape)
    for coord in range(2):
        rows = []
        for part in range(sz.parts):
            row = source_ref[coord : coord + 1, part * LANES : (part + 1) * LANES]
            pack_ref[coord * sz.parts + part : coord * sz.parts + part + 1, :] = row
            rows.append(row)
        at = sz.edge_row + coord
        pack_ref[at : at + 1, :] = lookup(rows, edges)[:1]
    slot = iota((SLOTS, sz.blobs), 0)
    member = jnp.where(slot < count_ref[...], member_ref[...], -1).astype(jnp.float32)
    pack_ref[sz.member_row : sz.member_row + HALF, :] = jnp.concatenate(
        [member[:HALF], member[HALF:]], axis=1
    )


def resolve_zone(sz, zone, cat_ref, stage_ref, col_ref):
    shape = (HALF, LANES)
    member = cat_ref[zone, sz.member_row : sz.member_row + HALF, :].astype(jnp.int32)
    if isinstance(zone, int):
        before, after = max(zone - 1, 0), min(zone + 1, sz.zones - 1)
    else:
        before, after = jnp.maximum(zone - 1, 0), jnp.minimum(zone + 1, sz.zones - 1)
    low = member < sz.edge
    high = member >= sz.edge + sz.sources
    own = jnp.clip(member - sz.edge, 0, sz.sources - 1)
    rim = jnp.where(
        low, sz.edge + jnp.maximum(member, 0), jnp.where(high, member - sz.edge - sz.sources, 0)
    )
    lane = iota(shape, 1)
    for coord in range(2):
        rows = [
            cat_ref[zone, coord * sz.parts + part : coord * sz.parts + part + 1, :]
            for part in range(sz.parts)
        ]
        at = sz.edge_row + coord
        table = jnp.where(
            lane >= sz.edge,
            spread_rows(cat_ref[before, at : at + 1, :], shape),
            spread_rows(cat_ref[after, at : at + 1, :], shape),
        )
        place = jnp.where(low | high, take(table, rim), lookup(rows, own))
        if coord == 0:
            place = jnp.where(member < 0, FAR, place)
            start = zone * HALF if isinstance(zone, int) else pl.multiple_of(zone * HALF, HALF)
            stage_ref[pl.ds(start, HALF), :] = place
        else:
            col_ref[zone] = place


def spread_zone(sz, zone, turned_ref, row_ref):
    shape = (8, LANES)
    lane = iota(shape, 1)
    per = LANES // HALF
    index = (zone % per) * HALF + lane % HALF
    upper = lane % SLOTS >= HALF
    for part in range(sz.blobs // 8):
        pieces = []
        for half in range(2):
            at = half * sz.blobs + part * 8
            pieces.append(take(turned_ref[zone // per, at : at + 8, :], index))
        start = zone * sz.blobs + part * 8
        if not isinstance(zone, int):
            start = pl.multiple_of(start, 8)
        row_ref[pl.ds(start, 8), :] = jnp.where(upper, pieces[1], pieces[0])


def prepare(sz, cat_ref, stage_ref, turned_ref, col_ref, row_ref):
    each = (lambda body: [body(z) for z in range(sz.zones)]) if sz.zones <= 8 else (
        lambda body: lax.fori_loop(0, sz.zones, lambda z, c: (body(z), c)[1], 0)
    )
    each(lambda z: resolve_zone(sz, z, cat_ref, stage_ref, col_ref))
    for part in range(turned_ref.shape[0]):
        turned_ref[part] = stage_ref[part * LANES : (part + 1) * LANES, :].T
    each(lambda z: spread_zone(sz, z, turned_ref, row_ref))


def split(value):
    head = value.astype(jnp.bfloat16)
    return head, (value - head.astype(jnp.float32)).astype(jnp.bfloat16)


def tile_batch(
    sz, step, per, blob_ref, band_ref, shift_ref, amp_ref, rate_ref, pixel_ref, weight_ref,
    col_ref, row_ref, line_ref, result_ref,
):
    height = pixel_ref.shape[1]
    eight = (HALF, LANES)
    shape = (SLOTS, LANES)
    lane = iota(eight, 1)
    sub = iota(eight, 0)
    sub_f = sub.astype(jnp.float32)
    lane_f = lane.astype(jnp.float32)
    slots_all = COMPS * SLOTS
    width = COMPS * HALF
    keep = (iota(shape, 1) % HALF == iota(shape, 0) % HALF) & (iota(shape, 1) < 3 * width)
    keep = jnp.where(keep, 1.0, 0.0).astype(jnp.bfloat16)
    comp = lane // SLOTS % COMPS
    high_part = (lane < width) | (lane >= 2 * width)
    half_index = lane // HALF % COMPS * SLOTS + lane % HALF
    seat_a = lane // HALF == sub
    seat_b = lane // HALF == sub + HALF
    blank = jnp.zeros((LANES - 3 * width, LANES), jnp.float32)
    zero_tail = jnp.zeros((slots_all, LANES), jnp.bfloat16)
    zero_rows = jnp.zeros((LANES - 2 * slots_all, 2 * LANES), jnp.bfloat16)

    for slot in range(per):
        tile = step * per + slot
        blob = blob_ref[0, tile]
        zone = lax.div(blob, sz.blobs)
        local = lax.rem(blob, sz.blobs)
        rate = [rate_ref[g, tile] for g in range(COMPS)]
        amp = [amp_ref[g, tile] for g in range(COMPS)]
        row_rate = jnp.where(comp == 0, rate[0], jnp.where(comp == 1, rate[1], rate[2]))
        row_amp = jnp.where(comp == 0, amp[0], jnp.where(comp == 1, amp[1], amp[2]))
        row_shift = shift_ref[0, tile]
        row_base = row_shift + spread_rows(row_ref[pl.ds(blob, 1), :], eight)
        col_base = shift_ref[1, tile]
        col_table = col_ref[zone]
        square = []
        for half in range(2):
            index = jnp.full(eight, half * sz.blobs, jnp.int32) + local
            away = lane_f - col_base - take(col_table, index)
            square.append(away * away)
        cols = [[jnp.exp2(rate[g] * square[half]) for half in range(2)] for g in range(COMPS)]
        heads, tails, heads_f, tails_f = [], [], [], []
        for g in range(COMPS):
            both = jnp.concatenate(cols[g], axis=0)
            head = both.astype(jnp.bfloat16)
            head_f = head.astype(jnp.float32)
            heads.append(head)
            heads_f.append(head_f)
            tails_f.append(both - head_f)
            tails.append(tails_f[-1].astype(jnp.bfloat16))
        rights = []
        for half in range(2):
            span = slice(half * HALF, (half + 1) * HALF)
            top = [h[span] for h in heads_f]
            rights.append(
                jnp.concatenate(top + top + [t[span] for t in tails_f] + [blank], axis=0).astype(
                    jnp.bfloat16
                )
            )
        rows = []
        for part in range(height // 8):
            away = (sub_f + 8.0 * part) - row_base
            value = jnp.exp2(row_rate * (away * away)) * row_amp
            rows.append(value)
            line_ref[slot, 0, part * 8 : (part + 1) * 8, :] = value
            for half in range(2):
                seen = take(value, half_index + half * HALF)
                head = seen.astype(jnp.bfloat16).astype(jnp.float32)
                line_ref[slot, 1 + half, part * 8 : (part + 1) * 8, :] = jnp.where(
                    high_part, head, seen - head
                )
        models = []
        for half in range(2):
            left = []
            for i in range(0, height, 2):
                pair = jnp.concatenate(
                    [
                        spread_rows(line_ref[slot, 1 + half, i + d : i + d + 1, :], eight)
                        for d in range(2)
                    ],
                    axis=0,
                )
                left.append(pair.astype(jnp.bfloat16) * keep)
            models.append(
                lax.dot_general(
                    jnp.concatenate(left, axis=0), rights[half], (((1,), (0,)), ((), ())),
                    preferred_element_type=jnp.float32,
                )
            )
        left = []
        for i in range(height):
            span = slice(i * HALF, (i + 1) * HALF)
            weight = spread_rows(weight_ref[tile, i : i + 1, :], shape)
            scaled = jnp.concatenate([models[0][span], models[1][span]], axis=0) * weight
            left.append(jnp.concatenate(split(scaled), axis=1))
        left.append(jnp.concatenate(split(weight_ref[tile] * pixel_ref[tile]), axis=1))
        top = jnp.concatenate(heads, axis=0)
        right = jnp.concatenate(
            [
                jnp.concatenate([top, top], axis=1),
                jnp.concatenate([jnp.concatenate(tails, axis=0), zero_tail], axis=1),
                zero_rows,
            ],
            axis=0,
        )
        product = lax.dot_general(
            jnp.concatenate(left, axis=0), right, (((1,), (1,)), ((), ())),
            preferred_element_type=jnp.float32,
        )
        normal = None
        for i in range(height):
            line = spread_rows(line_ref[slot, 0, i : i + 1, :], shape)
            term = product[i * SLOTS : (i + 1) * SLOTS] * line
            normal = term if normal is None else normal + term
        vector = None
        for part in range(height // 8):
            at = height * SLOTS + part * 8
            term = product[at : at + 8] * rows[part]
            vector = term if vector is None else vector + term
        folded = jnp.concatenate([normal, vector], axis=0)
        for shift in (LANES // 2, LANES // 4, LANES // 8):
            folded = folded + pltpu.roll(folded, shift, 1)
        upper, lower, vector = folded[:HALF], folded[HALF:SLOTS], folded[SLOTS:]
        step_back = SLOTS - HALF - 1
        main = jnp.where(
            seat_a, pltpu.roll(upper, 0, 1, stride=step_back, stride_axis=0),
            jnp.where(
                seat_b,
                pltpu.roll(lower, HALF * step_back, 1, stride=step_back, stride_axis=0), 0.0,
            ),
        )
        code = (
            lax.div(local, sz.share) * sz.systems
            + band_ref[0, tile] * sz.share
            + lax.rem(local, sz.share)
        )
        rest = jnp.where(lane == sub, pltpu.roll(upper, HALF, 1), 0.0)
        rest = jnp.where((lane >= SLOTS) & (lane < 2 * SLOTS), vector, rest)
        rest = jnp.where((lane == HALF) & (sub == 0), code.astype(jnp.float32), rest)
        result_ref[0, pl.ds(tile, 1), :] = jnp.sum(main, axis=0, keepdims=True)
        result_ref[1, pl.ds(tile, 1), :] = jnp.sum(rest, axis=0, keepdims=True)


def route_terms(sz, blob_ref, result_ref, terms_ref):
    square = (sz.tiles, sz.tiles)
    zone = spread_rows(lax.div(blob_ref[...], sz.blobs).astype(jnp.float32), square)
    same = (zone == zone.T) & (iota(square, 0) < iota(square, 1))
    rank = jnp.sum(jnp.where(same, 1.0, 0.0), axis=0, keepdims=True)
    place = zone[:1] * float(sz.capacity) + rank
    entry = iota((sz.entries, sz.tiles), 0).astype(jnp.float32)
    hit = jnp.where(entry == place, 1.0, 0.0).astype(jnp.bfloat16)
    left = jnp.concatenate([result_ref[0], result_ref[1]], axis=1)
    moved = None
    for _ in range(3):
        piece = left.astype(jnp.bfloat16)
        left = left - piece.astype(jnp.float32)
        part = lax.dot_general(
            hit, piece, (((1,), (0,)), ((), ())), preferred_element_type=jnp.float32
        )
        moved = part if moved is None else moved + part
    for number in range(sz.zones):
        start = number * sz.capacity
        terms_ref[number, : sz.capacity, :] = moved[start : start + sz.capacity, :LANES]
        total = None
        for seat in range(SEATS):
            at = start + seat * sz.rest
            piece = moved[at : at + sz.rest, LANES:]
            piece = pltpu.roll(piece, seat * SEAT, 1) if seat else piece
            total = piece if total is None else total + piece
        terms_ref[number, sz.capacity : sz.capacity + sz.rest, :] = total


def find_seats(sz, zone, cat_ref, edge_ref, seat_ref):
    shape = (HALF, LANES)
    edges = spread_rows(edge_ref[...], shape)
    source = iota((sz.sources, LANES), 0)
    lane = iota((1, LANES), 1)
    total = None
    for side in range(3):
        near = lax.rem(zone + side - 1 + sz.zones, sz.zones)
        member = cat_ref[near, sz.member_row : sz.member_row + HALF, :].astype(jnp.int32)
        top = sz.edge + sz.sources
        if side == 0:
            valid = (member >= top) & (zone > 0)
            target = take(edges, jnp.where(valid, member - top, 0))
        elif side == 1:
            valid = (member >= sz.edge) & (member < top)
            target = member - sz.edge
        else:
            valid = (member >= 0) & (member < sz.edge) & (zone < sz.zones - 1)
            target = take(edges, jnp.where(valid, member + sz.edge, 0))
        target = jnp.where(valid, target, -1)
        for row in range(HALF):
            hit = source == target[row : row + 1, :]
            right = jnp.where(hit, 1.0, 0.0).astype(jnp.bfloat16)
            slot = side * SLOTS + row + lane // sz.blobs * HALF
            left = jnp.concatenate(
                [slot, lane % sz.blobs, jnp.zeros((SLOTS - 2, LANES), jnp.int32)], axis=0
            )
            part = lax.dot_general(
                left.astype(jnp.float32).astype(jnp.bfloat16), right, (((1,), (1,)), ((), ())),
                preferred_element_type=jnp.float32,
            )
            total = part if total is None else total + part
    seat_ref[...] = total[:8].astype(jnp.int32)


def gather_terms(sz, got_ref, table_ref, part_ref):
    for zone in range(sz.zones):
        start = zone * sz.capacity
        table_ref[start : start + sz.capacity, :LANES] = got_ref[zone, : sz.capacity, :]
        rest = got_ref[zone, sz.capacity : sz.capacity + sz.rest, :]
        for seat in range(SEATS):
            at = start + seat * sz.rest
            table_ref[at : at + sz.rest, LANES:] = (
                pltpu.roll(rest, LANES - seat * SEAT, 1) if seat else rest
            )
    square = (LANES, LANES)
    diagonal = iota(square, 0) == iota(square, 1)
    codes = []
    for at in range(0, sz.entries, LANES):
        block = table_ref[at : at + LANES, LANES:]
        code = take(block, jnp.full(square, HALF, jnp.int32))
        codes.append(jnp.sum(jnp.where(diagonal, code, 0.0), axis=0, keepdims=True))
    codes = jnp.concatenate(codes, axis=1)
    count = sz.bands * sz.block
    system = iota((count, sz.entries), 0)
    hit = jnp.where(system.astype(jnp.float32) == codes, 1.0, 0.0).astype(jnp.bfloat16)
    head, tail = split(table_ref[...])
    dims = (((1,), (0,)), ((), ()))
    total = lax.dot_general(hit, head, dims, preferred_element_type=jnp.float32)
    total = total + lax.dot_general(hit, tail, dims, preferred_element_type=jnp.float32)
    lane = iota((sz.third, LANES), 1) // SEAT
    for owner in range(sz.bands):
        start = owner * sz.block
        part_ref[owner, : sz.block, :] = total[start : start + sz.block, :LANES]
        rest = None
        for seat in range(FILTER_BANDS):
            at = start + seat * sz.third
            piece = total[at : at + sz.third, LANES:]
            piece = jnp.where(lane == seat, pltpu.roll(piece, seat * SEAT, 1) if seat else piece, 0.0)
            rest = piece if rest is None else rest + piece
        part_ref[owner, sz.block :, :] = rest


def solve(sz, summed, flat_ref, square_ref):
    main, rest = summed[: sz.block], summed[sz.block :]
    rest = jnp.concatenate(
        [pltpu.roll(rest, LANES - s * SEAT, 1) if s else rest for s in range(FILTER_BANDS)], axis=0
    )
    fill = jnp.zeros((LANES - sz.block, LANES), jnp.float32)
    flat_ref[:LANES, :] = jnp.concatenate([main, fill], axis=0).T
    flat_ref[LANES:, :] = jnp.concatenate([rest, fill], axis=0).T[: 2 * SLOTS]
    for l in range(SLOTS):
        for j in range(SLOTS):
            away = (l - j) % SLOTS
            if away < HALF:
                at = HALF * j + away
            elif away == HALF:
                at = LANES + min(j, l)
            else:
                at = HALF * l + SLOTS - away
            square_ref[l, j : j + 1, :] = flat_ref[at : at + 1, :]
    shape = (SLOTS, LANES)
    sub = iota(shape, 0)
    columns = [square_ref[l] + jnp.where(sub == l, PRIOR, 0.0) for l in range(SLOTS)]
    columns.append(flat_ref[LANES + SLOTS : LANES + 2 * SLOTS, :])
    scale = columns[0]
    for k in range(SLOTS):
        column = columns[k]
        inverse = 1.0 / column[k : k + 1]
        scale = jnp.where(sub == k, column, scale)
        column = jnp.where(sub == k, 0.0, column)
        for l in range(k + 1, SLOTS + 1):
            ratio = columns[l][k : k + 1] * inverse
            columns[l] = columns[l] - column * ratio
    return columns[SLOTS] / scale


def whole_kernel(
    sz, per,
    pixel_hbm, weight_hbm, blob_ref, band_ref, shift_ref, amp_ref, sigma_ref, blob_row_ref,
    source_ref, edge_ref, member_ref, count_ref, out_ref,
    pixel_ref, weight_ref, rate_row_ref, rate_ref, pack_ref, cat_ref,
    stage_ref, turned_ref, col_ref, row_ref, line_ref, result_ref, terms_ref,
    got_ref, table_ref, part_ref, sum_ref, flat_ref, square_ref, solved_ref, flux_ref, seat_ref,
    load_sem, send_cat, recv_cat, own_cat,
    send_term, recv_term, own_term, send_sum, recv_sum, send_flux, recv_flux,
):
    zones, bands = sz.zones, sz.bands
    zone = lax.axis_index("zone")
    band = lax.axis_index("band")
    at = lambda dz, db: (lax.rem(zone + dz + zones, zones), lax.rem(band + db, bands))
    far = [(partner(zone, step, zones), band) for step in range(zones - 1, 0, -1)]
    near = [at(0, db) for db in range(1, bands)]
    above, below = zone < zones - 1, zone > 0
    beside = [(1, above, below), (-1, below, above)]
    barrier = pltpu.get_barrier_semaphore()

    def greet(target):
        pl.semaphore_signal(barrier, inc=1, device_id=target, device_id_type=MESH)

    for target in far + near:
        greet(target)
    for dz, sends, _ in beside:

        @pl.when(sends)
        def _():
            for db in range(1, bands):
                greet(at(dz, db))

    loads = [
        pltpu.make_async_copy(pixel_hbm, pixel_ref, load_sem.at[0]),
        pltpu.make_async_copy(weight_hbm, weight_ref, load_sem.at[1]),
    ]
    for copy in loads:
        copy.start()
    sigma = sigma_ref[...]
    rate_row_ref[...] = (-0.5 * LOG2E) / (sigma * sigma)
    pack_catalog(sz, source_ref, edge_ref, member_ref, count_ref, pack_ref)
    loads.append(pltpu.make_async_copy(rate_row_ref, rate_ref, load_sem.at[2]))
    loads[-1].start()
    sent = pl.ds(0, sz.sent_rows)
    own = pltpu.make_async_copy(pack_ref.at[sent], cat_ref.at[zone, sent], own_cat)
    own.start()
    ends = lax.div(zone, zones - 1) + lax.div(zones - 1 - zone, zones - 1)
    pl.semaphore_wait(barrier, len(far) + len(near) + (bands - 1) * (2 - ends))
    copies = []
    for order, target in enumerate(far):
        copy = pltpu.make_async_remote_copy(
            src_ref=pack_ref.at[sent],
            dst_ref=cat_ref.at[zone, sent],
            send_sem=send_cat.at[order],
            recv_sem=recv_cat.at[order],
            device_id=target,
            device_id_type=MESH,
        )
        copy.start()
        copies.append(copy)
    for copy in loads:
        copy.wait()
    own.wait()
    for copy in copies:
        copy.wait()
    prepare(sz, cat_ref, stage_ref, turned_ref, col_ref, row_ref)

    def body(step, carry):
        tile_batch(
            sz, step, per, blob_ref, band_ref, shift_ref, amp_ref, rate_ref,
            pixel_ref, weight_ref, col_ref, row_ref, line_ref, result_ref,
        )
        return carry

    lax.fori_loop(0, sz.tiles // per, body, 0)
    route_terms(sz, blob_row_ref, result_ref, terms_ref)
    own = pltpu.make_async_copy(terms_ref.at[zone], got_ref.at[zone], own_term)
    own.start()
    copies = []
    for order, target in enumerate(far):
        copy = pltpu.make_async_remote_copy(
            src_ref=terms_ref.at[target[0]],
            dst_ref=got_ref.at[zone],
            send_sem=send_term.at[order],
            recv_sem=recv_term.at[order],
            device_id=target,
            device_id_type=MESH,
        )
        copy.start()
        copies.append(copy)
    find_seats(sz, zone, cat_ref, edge_ref, seat_ref)
    own.wait()
    for copy in copies:
        copy.wait()

    gather_terms(sz, got_ref, table_ref, part_ref)
    copies = []
    for order, target in enumerate(near):
        copy = pltpu.make_async_remote_copy(
            src_ref=part_ref.at[target[1]],
            dst_ref=sum_ref.at[order],
            send_sem=send_sum.at[order],
            recv_sem=recv_sum.at[order],
            device_id=target,
            device_id_type=MESH,
        )
        copy.start()
        copies.append(copy)
    for copy in copies:
        copy.wait()
    summed = part_ref[band]
    for order in range(len(near)):
        summed = summed + sum_ref[order]
    solved = solve(sz, summed, flat_ref, square_ref)
    eight = (HALF, LANES)
    packed = jnp.where(
        iota(eight, 1) < LANES // 2, solved[:HALF], pltpu.roll(solved[HALF:], LANES // 2, 1)
    )
    solved_ref[...] = packed
    flux_ref[bands + band] = packed

    def flux_copy(order, side, target):
        return pltpu.make_async_remote_copy(
            src_ref=solved_ref,
            dst_ref=flux_ref.at[side * bands + band],
            send_sem=send_flux.at[order],
            recv_sem=recv_flux.at[order],
            device_id=target,
            device_id_type=MESH,
        )

    across = []
    for number, (dz, sends, receives) in enumerate(beside):
        first = bands - 1 + number * bands
        group = [flux_copy(first + db, 1 - dz, at(dz, db)) for db in range(bands)]
        across.append((group, sends, receives))

        @pl.when(sends)
        def _():
            for copy in group:
                copy.start()

    copies = [flux_copy(order, 1, target) for order, target in enumerate(near)]
    for copy in copies:
        copy.start()
    for copy in copies:
        copy.wait()
    for group, sends, receives in across:

        @pl.when(sends)
        def _():
            for copy in group:
                copy.wait_send()

        @pl.when(receives)
        def _():
            for copy in group:
                copy.wait_recv()

    sub = iota(eight, 0)
    for part in range(sz.parts):
        span = slice(part * LANES, (part + 1) * LANES)
        slot = spread_rows(seat_ref[0:1, span], eight)
        blob = spread_rows(seat_ref[1:2, span], eight)
        row = slot % SLOTS
        key = slot // SLOTS * bands + blob // sz.share
        index = row // HALF * (LANES // 2) + blob % sz.share
        key = jnp.where(sub == row % HALF, key, -1)
        values = [jnp.zeros(eight, jnp.float32) for _ in range(FILTER_BANDS)]
        for table in range(3 * bands):
            flux = flux_ref[table]
            hit = key == table
            for k in range(FILTER_BANDS):
                values[k] = jnp.where(hit, take(flux, index + k * sz.share), values[k])
        out_ref[:, span] = jnp.concatenate(
            [jnp.sum(value, axis=0, keepdims=True) for value in values], axis=0
        )


def on_device(
    sizes, pixels, inv_var, tile_offset, psf_amp, psf_sigma, tile_blob, tile_band,
    source_pos, edge_rows, blob_members, sources_per_blob,
):
    zones, bands = sizes
    sz = Sizes(
        zones, bands, source_pos.shape[1], edge_rows.shape[0] // 2,
        sources_per_blob.shape[0], pixels.shape[0],
    )
    dma = pltpu.SemaphoreType.DMA
    f32 = jnp.float32
    tiles, height, width = pixels.shape
    per = TILES_STEP
    while tiles % per:
        per -= 1
    turned = -(-zones * HALF // LANES)
    near = 3 * bands - 1
    rows = sz.block + sz.third
    blob_row = tile_blob.reshape(1, -1)
    return pl.pallas_call(
        functools.partial(whole_kernel, sz, per),
        out_shape=jax.ShapeDtypeStruct((FILTER_BANDS, sz.sources), f32),
        in_specs=[ANY] * 2 + [SMEM] * 4 + [VMEM] * 6,
        out_specs=VMEM,
        scratch_shapes=[
            pltpu.VMEM((tiles, height, width), f32),
            pltpu.VMEM((tiles, height, width), f32),
            pltpu.VMEM((COMPS, tiles), f32),
            pltpu.SMEM((COMPS, tiles), f32),
            pltpu.VMEM((sz.cat_rows, LANES), f32),
            pltpu.VMEM((zones, sz.cat_rows, LANES), f32),
            pltpu.VMEM((turned * LANES, LANES), f32),
            pltpu.VMEM((turned, LANES, LANES), f32),
            pltpu.VMEM((zones, HALF, LANES), f32),
            pltpu.VMEM((zones * sz.blobs, LANES), f32),
            pltpu.VMEM((per, 3, height, width), f32),
            pltpu.VMEM((2, tiles, LANES), f32),
            pltpu.VMEM((zones, sz.rows, LANES), f32),
            pltpu.VMEM((zones, sz.rows, LANES), f32),
            pltpu.VMEM((sz.entries, 2 * LANES), f32),
            pltpu.VMEM((bands, rows, LANES), f32),
            pltpu.VMEM((bands - 1, rows, LANES), f32),
            pltpu.VMEM((LANES + 2 * SLOTS, LANES), f32),
            pltpu.VMEM((SLOTS, SLOTS, LANES), f32),
            pltpu.VMEM((HALF, LANES), f32),
            pltpu.VMEM((3 * bands, HALF, LANES), f32),
            pltpu.VMEM((8, sz.sources), jnp.int32),
            dma((3,)), dma((zones - 1,)), dma((zones - 1,)), dma,
            dma((zones - 1,)), dma((zones - 1,)), dma,
            dma((bands - 1,)), dma((bands - 1,)),
            dma((near,)), dma((near,)),
        ],
        compiler_params=pltpu.CompilerParams(
            collective_id=0, has_side_effects=True,
        ),
    )(
        pixels, inv_var, blob_row, tile_band.reshape(1, -1), tile_offset, psf_amp, psf_sigma,
        blob_row, source_pos, edge_rows.reshape(1, -1), blob_members.T,
        sources_per_blob.reshape(1, -1),
    )


def solution(mesh):
    sizes = (mesh.shape["zone"], mesh.shape["band"])
    return jax.shard_map(
        functools.partial(on_device, sizes),
        mesh=mesh,
        in_specs=(
            P(("zone", "band"), None, None),
            P(("zone", "band"), None, None),
            P(None, ("zone", "band")),
            P(None, ("zone", "band")),
            P(None, ("zone", "band")),
            P(("zone", "band")),
            P(("zone", "band")),
            P(None, "zone"),
            P("zone"),
            P("zone", None),
            P("zone"),
        ),
        out_specs=P(None, "zone"),
        check_vma=False,
    )
```

```python
import functools
import math

import jax
import jax.numpy as jnp
from jax import lax
from jax.experimental import pallas as pl
from jax.experimental.pallas import tpu as pltpu
from jax.sharding import PartitionSpec as P

FILTER_BANDS = 3
COMPS = 3
SLOTS = 16
HALF = SLOTS // 2
LANES = 128
SEATS = 4
SEAT = LANES // SEATS
TILES_STEP = 32
PRIOR = 1.0
FAR = 1.0e4
LOG2E = math.log2(math.e)

VMEM = pl.BlockSpec(memory_space=pltpu.VMEM)
SMEM = pl.BlockSpec(memory_space=pltpu.SMEM)
ANY = pl.BlockSpec(memory_space=pl.ANY)
MESH = pl.DeviceIdType.MESH


def iota(shape, axis):
    return lax.broadcasted_iota(jnp.int32, shape, axis)


def take(table, index):
    return jnp.take_along_axis(table, index, axis=1, mode="promise_in_bounds")


def spread_rows(row, shape):
    return jnp.broadcast_to(row, shape)


def lookup(rows, index):
    found = jnp.zeros(index.shape, rows[0].dtype)
    low = index & (LANES - 1)
    for part, row in enumerate(rows):
        hit = take(spread_rows(row, index.shape), low)
        found = jnp.where(index // LANES == part, hit, found)
    return found


def partner(zone, step, zones):
    if zones & (zones - 1):
        return lax.rem(zone + step, zones)
    other = 0
    bit = 1
    while bit < zones:
        digit = lax.rem(lax.div(zone, bit), 2)
        other = other + bit * ((1 - digit) if step & bit else digit)
        bit *= 2
    return other


class Sizes:
    def __init__(self, zones, bands, sources, edge, blobs, tiles):
        self.zones, self.bands = zones, bands
        self.sources, self.edge, self.blobs, self.tiles = sources, edge, blobs, tiles
        self.parts = sources // LANES
        self.member_row = -(-2 * self.parts // 8) * 8
        self.edge_row = self.member_row + HALF
        self.cat_rows = self.edge_row + 8
        self.sent_rows = self.edge_row + 2
        capacity = max(SEATS, (2 * tiles + zones - 1) // zones)
        self.capacity = -(-capacity // SEATS) * SEATS
        self.rest = self.capacity // SEATS
        self.rows = -(-(self.capacity + self.rest) // 8) * 8
        self.share = blobs // bands
        self.systems = FILTER_BANDS * self.share
        self.block = -(-self.systems // 8) * 8
        self.third = self.block // FILTER_BANDS
        self.entries = zones * self.capacity


def pack_catalog(sz, source_ref, edge_ref, member_ref, count_ref, pack_ref):
    shape = (8, LANES)
    edges = spread_rows(edge_ref[...], shape)
    for coord in range(2):
        rows = []
        for part in range(sz.parts):
            row = source_ref[coord : coord + 1, part * LANES : (part + 1) * LANES]
            pack_ref[coord * sz.parts + part : coord * sz.parts + part + 1, :] = row
            rows.append(row)
        at = sz.edge_row + coord
        pack_ref[at : at + 1, :] = lookup(rows, edges)[:1]
    slot = iota((SLOTS, sz.blobs), 0)
    member = jnp.where(slot < count_ref[...], member_ref[...], -1).astype(jnp.float32)
    pack_ref[sz.member_row : sz.member_row + HALF, :] = jnp.concatenate(
        [member[:HALF], member[HALF:]], axis=1
    )


def resolve_zone(sz, zone, cat_ref, stage_ref, col_ref):
    shape = (HALF, LANES)
    member = cat_ref[zone, sz.member_row : sz.member_row + HALF, :].astype(jnp.int32)
    if isinstance(zone, int):
        before, after = max(zone - 1, 0), min(zone + 1, sz.zones - 1)
    else:
        before, after = jnp.maximum(zone - 1, 0), jnp.minimum(zone + 1, sz.zones - 1)
    low = member < sz.edge
    high = member >= sz.edge + sz.sources
    own = jnp.clip(member - sz.edge, 0, sz.sources - 1)
    rim = jnp.where(
        low, sz.edge + jnp.maximum(member, 0), jnp.where(high, member - sz.edge - sz.sources, 0)
    )
    lane = iota(shape, 1)
    for coord in range(2):
        rows = [
            cat_ref[zone, coord * sz.parts + part : coord * sz.parts + part + 1, :]
            for part in range(sz.parts)
        ]
        at = sz.edge_row + coord
        table = jnp.where(
            lane >= sz.edge,
            spread_rows(cat_ref[before, at : at + 1, :], shape),
            spread_rows(cat_ref[after, at : at + 1, :], shape),
        )
        place = jnp.where(low | high, take(table, rim), lookup(rows, own))
        if coord == 0:
            place = jnp.where(member < 0, FAR, place)
            start = zone * HALF if isinstance(zone, int) else pl.multiple_of(zone * HALF, HALF)
            stage_ref[pl.ds(start, HALF), :] = place
        else:
            col_ref[zone] = place


def spread_zone(sz, zone, turned_ref, row_ref):
    shape = (8, LANES)
    lane = iota(shape, 1)
    per = LANES // HALF
    index = (zone % per) * HALF + lane % HALF
    upper = lane % SLOTS >= HALF
    for part in range(sz.blobs // 8):
        pieces = []
        for half in range(2):
            at = half * sz.blobs + part * 8
            pieces.append(take(turned_ref[zone // per, at : at + 8, :], index))
        start = zone * sz.blobs + part * 8
        if not isinstance(zone, int):
            start = pl.multiple_of(start, 8)
        row_ref[pl.ds(start, 8), :] = jnp.where(upper, pieces[1], pieces[0])


def prepare(sz, cat_ref, stage_ref, turned_ref, col_ref, row_ref):
    each = (lambda body: [body(z) for z in range(sz.zones)]) if sz.zones <= 8 else (
        lambda body: lax.fori_loop(0, sz.zones, lambda z, c: (body(z), c)[1], 0)
    )
    each(lambda z: resolve_zone(sz, z, cat_ref, stage_ref, col_ref))
    for part in range(turned_ref.shape[0]):
        turned_ref[part] = stage_ref[part * LANES : (part + 1) * LANES, :].T
    each(lambda z: spread_zone(sz, z, turned_ref, row_ref))


def split(value):
    head = value.astype(jnp.bfloat16)
    return head, (value - head.astype(jnp.float32)).astype(jnp.bfloat16)


def tile_batch(
    sz, step, per, blob_ref, band_ref, shift_ref, amp_ref, rate_ref, pixel_ref, weight_ref,
    col_ref, row_ref, line_ref, result_ref,
):
    height = pixel_ref.shape[1]
    eight = (HALF, LANES)
    shape = (SLOTS, LANES)
    lane = iota(eight, 1)
    sub = iota(eight, 0)
    sub_f = sub.astype(jnp.float32)
    lane_f = lane.astype(jnp.float32)
    slots_all = COMPS * SLOTS
    width = COMPS * HALF
    keep = (iota(shape, 1) % HALF == iota(shape, 0) % HALF) & (iota(shape, 1) < 3 * width)
    keep = jnp.where(keep, 1.0, 0.0).astype(jnp.bfloat16)
    comp = lane // SLOTS % COMPS
    high_part = (lane < width) | (lane >= 2 * width)
    half_index = lane // HALF % COMPS * SLOTS + lane % HALF
    seat_a = lane // HALF == sub
    seat_b = lane // HALF == sub + HALF
    blank = jnp.zeros((LANES - 3 * width, LANES), jnp.float32)
    zero_tail = jnp.zeros((slots_all, LANES), jnp.bfloat16)
    zero_rows = jnp.zeros((LANES - 2 * slots_all, LANES), jnp.bfloat16)
    pending = []

    for slot in range(per):
        tile = step * per + slot
        blob = blob_ref[0, tile]
        zone = lax.div(blob, sz.blobs)
        local = lax.rem(blob, sz.blobs)
        rate = [rate_ref[g, tile] for g in range(COMPS)]
        amp = [amp_ref[g, tile] for g in range(COMPS)]
        row_rate = jnp.where(comp == 0, rate[0], jnp.where(comp == 1, rate[1], rate[2]))
        row_amp = jnp.where(comp == 0, amp[0], jnp.where(comp == 1, amp[1], amp[2]))
        row_shift = shift_ref[0, tile]
        row_base = row_shift + spread_rows(row_ref[pl.ds(blob, 1), :], eight)
        col_base = shift_ref[1, tile]
        col_table = col_ref[zone]
        square = []
        for half in range(2):
            index = jnp.full(eight, half * sz.blobs, jnp.int32) + local
            away = lane_f - col_base - take(col_table, index)
            square.append(away * away)
        cols = [[jnp.exp2(rate[g] * square[half]) for half in range(2)] for g in range(COMPS)]
        heads, tails, heads_f, tails_f = [], [], [], []
        for g in range(COMPS):
            both = jnp.concatenate(cols[g], axis=0)
            head = both.astype(jnp.bfloat16)
            head_f = head.astype(jnp.float32)
            heads.append(head)
            heads_f.append(head_f)
            tails_f.append(both - head_f)
            tails.append(tails_f[-1].astype(jnp.bfloat16))
        rights = []
        for half in range(2):
            span = slice(half * HALF, (half + 1) * HALF)
            top = [h[span] for h in heads_f]
            rights.append(
                jnp.concatenate(top + top + [t[span] for t in tails_f] + [blank], axis=0).astype(
                    jnp.bfloat16
                )
            )
        rows = []
        for part in range(height // 8):
            away = (sub_f + 8.0 * part) - row_base
            value = jnp.exp2(row_rate * (away * away)) * row_amp
            rows.append(value)
            line_ref[slot, 0, part * 8 : (part + 1) * 8, :] = value
            for half in range(2):
                seen = take(value, half_index + half * HALF)
                head = seen.astype(jnp.bfloat16).astype(jnp.float32)
                line_ref[slot, 1 + half, part * 8 : (part + 1) * 8, :] = jnp.where(
                    high_part, head, seen - head
                )
        models = []
        for half in range(2):
            left = []
            for i in range(0, height, 2):
                pair = jnp.concatenate(
                    [
                        spread_rows(line_ref[slot, 1 + half, i + d : i + d + 1, :], eight)
                        for d in range(2)
                    ],
                    axis=0,
                )
                left.append(pair.astype(jnp.bfloat16) * keep)
            models.append(
                lax.dot_general(
                    jnp.concatenate(left, axis=0), rights[half], (((1,), (0,)), ((), ())),
                    preferred_element_type=jnp.float32,
                )
            )
        heads_left = []
        tails_left = []
        for i in range(height):
            span = slice(i * HALF, (i + 1) * HALF)
            weight = spread_rows(weight_ref[tile, i : i + 1, :], shape)
            scaled = jnp.concatenate([models[0][span], models[1][span]], axis=0) * weight
            head, tail = split(scaled)
            heads_left.append(head)
            tails_left.append(tail)
        head, tail = split(weight_ref[tile] * pixel_ref[tile])
        heads_left.append(head)
        tails_left.append(tail)
        top = jnp.concatenate(heads, axis=0)
        low = jnp.concatenate(tails, axis=0)
        pending.append((tile, blob, local, slot, rows, heads_left, tails_left, top, low))
        if len(pending) < 2:
            continue
        left = [
            jnp.concatenate([pending[0][5][i], pending[1][5][i], pending[0][6][i], pending[1][6][i]], axis=1)
            for i in range(height + 1)
        ]
        zero = zero_tail
        right = jnp.concatenate(
            [
                jnp.concatenate([pending[0][7], zero, pending[0][7], zero], axis=1),
                jnp.concatenate([pending[0][8], zero, zero, zero], axis=1),
                jnp.concatenate([zero_rows] * 4, axis=1),
                jnp.concatenate([zero, pending[1][7], zero, pending[1][7]], axis=1),
                jnp.concatenate([zero, pending[1][8], zero, zero], axis=1),
                jnp.concatenate([zero_rows] * 4, axis=1),
            ],
            axis=0,
        )
        product = lax.dot_general(
            jnp.concatenate(left, axis=0), right, (((1,), (1,)), ((), ())),
            preferred_element_type=jnp.float32,
        )
        for member in range(2):
            tile, blob, local, held, rows = pending[member][:5]
            side = slice(member * LANES, (member + 1) * LANES)
            normal = None
            for i in range(height):
                line = spread_rows(line_ref[held, 0, i : i + 1, :], shape)
                term = product[i * SLOTS : (i + 1) * SLOTS, side] * line
                normal = term if normal is None else normal + term
            vector = None
            for part in range(height // 8):
                at = height * SLOTS + part * 8
                term = product[at : at + 8, side] * rows[part]
                vector = term if vector is None else vector + term
            folded = jnp.concatenate([normal, vector], axis=0)
            for shift in (LANES // 2, LANES // 4, LANES // 8):
                folded = folded + pltpu.roll(folded, shift, 1)
            upper, lower, vector = folded[:HALF], folded[HALF:SLOTS], folded[SLOTS:]
            step_back = SLOTS - HALF - 1
            main = jnp.where(
                seat_a, pltpu.roll(upper, 0, 1, stride=step_back, stride_axis=0),
                jnp.where(
                    seat_b,
                    pltpu.roll(lower, HALF * step_back, 1, stride=step_back, stride_axis=0), 0.0,
                ),
            )
            code = (
                lax.div(local, sz.share) * sz.systems
                + band_ref[0, tile] * sz.share
                + lax.rem(local, sz.share)
            )
            rest = jnp.where(lane == sub, pltpu.roll(upper, HALF, 1), 0.0)
            rest = jnp.where((lane >= SLOTS) & (lane < 2 * SLOTS), vector, rest)
            rest = jnp.where((lane == HALF) & (sub == 0), code.astype(jnp.float32), rest)
            result_ref[0, pl.ds(tile, 1), :] = jnp.sum(main, axis=0, keepdims=True)
            result_ref[1, pl.ds(tile, 1), :] = jnp.sum(rest, axis=0, keepdims=True)
        pending = []


def route_terms(sz, blob_ref, result_ref, terms_ref):
    square = (sz.tiles, sz.tiles)
    zone = spread_rows(lax.div(blob_ref[...], sz.blobs).astype(jnp.float32), square)
    same = (zone == zone.T) & (iota(square, 0) < iota(square, 1))
    rank = jnp.sum(jnp.where(same, 1.0, 0.0), axis=0, keepdims=True)
    place = zone[:1] * float(sz.capacity) + rank
    entry = iota((sz.entries, sz.tiles), 0).astype(jnp.float32)
    hit = jnp.where(entry == place, 1.0, 0.0).astype(jnp.bfloat16)
    left = jnp.concatenate([result_ref[0], result_ref[1]], axis=1)
    moved = None
    for _ in range(3):
        piece = left.astype(jnp.bfloat16)
        left = left - piece.astype(jnp.float32)
        part = lax.dot_general(
            hit, piece, (((1,), (0,)), ((), ())), preferred_element_type=jnp.float32
        )
        moved = part if moved is None else moved + part
    for number in range(sz.zones):
        start = number * sz.capacity
        terms_ref[number, : sz.capacity, :] = moved[start : start + sz.capacity, :LANES]
        total = None
        for seat in range(SEATS):
            at = start + seat * sz.rest
            piece = moved[at : at + sz.rest, LANES:]
            piece = pltpu.roll(piece, seat * SEAT, 1) if seat else piece
            total = piece if total is None else total + piece
        terms_ref[number, sz.capacity : sz.capacity + sz.rest, :] = total


def find_seats(sz, zone, cat_ref, edge_ref, seat_ref):
    shape = (HALF, LANES)
    edges = spread_rows(edge_ref[...], shape)
    source = iota((sz.sources, LANES), 0)
    lane = iota((1, LANES), 1)
    total = None
    for side in range(3):
        near = lax.rem(zone + side - 1 + sz.zones, sz.zones)
        member = cat_ref[near, sz.member_row : sz.member_row + HALF, :].astype(jnp.int32)
        top = sz.edge + sz.sources
        if side == 0:
            valid = (member >= top) & (zone > 0)
            target = take(edges, jnp.where(valid, member - top, 0))
        elif side == 1:
            valid = (member >= sz.edge) & (member < top)
            target = member - sz.edge
        else:
            valid = (member >= 0) & (member < sz.edge) & (zone < sz.zones - 1)
            target = take(edges, jnp.where(valid, member + sz.edge, 0))
        target = jnp.where(valid, target, -1)
        for row in range(HALF):
            hit = source == target[row : row + 1, :]
            right = jnp.where(hit, 1.0, 0.0).astype(jnp.bfloat16)
            slot = side * SLOTS + row + lane // sz.blobs * HALF
            left = jnp.concatenate(
                [slot, lane % sz.blobs, jnp.zeros((SLOTS - 2, LANES), jnp.int32)], axis=0
            )
            part = lax.dot_general(
                left.astype(jnp.float32).astype(jnp.bfloat16), right, (((1,), (1,)), ((), ())),
                preferred_element_type=jnp.float32,
            )
            total = part if total is None else total + part
    seat_ref[...] = total[:8].astype(jnp.int32)


def gather_terms(sz, got_ref, table_ref, part_ref):
    for zone in range(sz.zones):
        start = zone * sz.capacity
        table_ref[start : start + sz.capacity, :LANES] = got_ref[zone, : sz.capacity, :]
        rest = got_ref[zone, sz.capacity : sz.capacity + sz.rest, :]
        for seat in range(SEATS):
            at = start + seat * sz.rest
            table_ref[at : at + sz.rest, LANES:] = (
                pltpu.roll(rest, LANES - seat * SEAT, 1) if seat else rest
            )
    square = (LANES, LANES)
    diagonal = iota(square, 0) == iota(square, 1)
    codes = []
    for at in range(0, sz.entries, LANES):
        block = table_ref[at : at + LANES, LANES:]
        code = take(block, jnp.full(square, HALF, jnp.int32))
        codes.append(jnp.sum(jnp.where(diagonal, code, 0.0), axis=0, keepdims=True))
    codes = jnp.concatenate(codes, axis=1)
    count = sz.bands * sz.block
    system = iota((count, sz.entries), 0)
    hit = jnp.where(system.astype(jnp.float32) == codes, 1.0, 0.0).astype(jnp.bfloat16)
    head, tail = split(table_ref[...])
    dims = (((1,), (0,)), ((), ()))
    total = lax.dot_general(hit, head, dims, preferred_element_type=jnp.float32)
    total = total + lax.dot_general(hit, tail, dims, preferred_element_type=jnp.float32)
    lane = iota((sz.third, LANES), 1) // SEAT
    for owner in range(sz.bands):
        start = owner * sz.block
        part_ref[owner, : sz.block, :] = total[start : start + sz.block, :LANES]
        rest = None
        for seat in range(FILTER_BANDS):
            at = start + seat * sz.third
            piece = total[at : at + sz.third, LANES:]
            piece = jnp.where(lane == seat, pltpu.roll(piece, seat * SEAT, 1) if seat else piece, 0.0)
            rest = piece if rest is None else rest + piece
        part_ref[owner, sz.block :, :] = rest


def solve(sz, summed, flat_ref, square_ref):
    main, rest = summed[: sz.block], summed[sz.block :]
    rest = jnp.concatenate(
        [pltpu.roll(rest, LANES - s * SEAT, 1) if s else rest for s in range(FILTER_BANDS)], axis=0
    )
    fill = jnp.zeros((LANES - sz.block, LANES), jnp.float32)
    flat_ref[:LANES, :] = jnp.concatenate([main, fill], axis=0).T
    flat_ref[LANES:, :] = jnp.concatenate([rest, fill], axis=0).T[: 2 * SLOTS]
    for l in range(SLOTS):
        for j in range(SLOTS):
            away = (l - j) % SLOTS
            if away < HALF:
                at = HALF * j + away
            elif away == HALF:
                at = LANES + min(j, l)
            else:
                at = HALF * l + SLOTS - away
            square_ref[l, j : j + 1, :] = flat_ref[at : at + 1, :]
    shape = (SLOTS, LANES)
    sub = iota(shape, 0)
    columns = [square_ref[l] + jnp.where(sub == l, PRIOR, 0.0) for l in range(SLOTS)]
    columns.append(flat_ref[LANES + SLOTS : LANES + 2 * SLOTS, :])
    scale = columns[0]
    for k in range(SLOTS):
        column = columns[k]
        inverse = 1.0 / column[k : k + 1]
        scale = jnp.where(sub == k, column, scale)
        column = jnp.where(sub == k, 0.0, column)
        for l in range(k + 1, SLOTS + 1):
            ratio = columns[l][k : k + 1] * inverse
            columns[l] = columns[l] - column * ratio
    return columns[SLOTS] / scale


def whole_kernel(
    sz, per,
    pixel_hbm, weight_hbm, blob_ref, band_ref, shift_ref, amp_ref, sigma_ref, blob_row_ref,
    source_ref, edge_ref, member_ref, count_ref, out_ref,
    pixel_ref, weight_ref, rate_row_ref, rate_ref, pack_ref, cat_ref,
    stage_ref, turned_ref, col_ref, row_ref, line_ref, result_ref, terms_ref,
    got_ref, table_ref, part_ref, sum_ref, flat_ref, square_ref, solved_ref, flux_ref, seat_ref,
    load_sem, send_cat, recv_cat, own_cat,
    send_term, recv_term, own_term, send_sum, recv_sum, send_flux, recv_flux,
):
    zones, bands = sz.zones, sz.bands
    zone = lax.axis_index("zone")
    band = lax.axis_index("band")
    at = lambda dz, db: (lax.rem(zone + dz + zones, zones), lax.rem(band + db, bands))
    far = [(partner(zone, step, zones), band) for step in range(zones - 1, 0, -1)]
    near = [at(0, db) for db in range(1, bands)]
    above, below = zone < zones - 1, zone > 0
    beside = [(1, above, below), (-1, below, above)]
    barrier = pltpu.get_barrier_semaphore()

    def greet(target):
        pl.semaphore_signal(barrier, inc=1, device_id=target, device_id_type=MESH)

    for target in far + near:
        greet(target)
    for dz, sends, _ in beside:

        @pl.when(sends)
        def _():
            for db in range(1, bands):
                greet(at(dz, db))

    loads = [
        pltpu.make_async_copy(pixel_hbm, pixel_ref, load_sem.at[0]),
        pltpu.make_async_copy(weight_hbm, weight_ref, load_sem.at[1]),
    ]
    for copy in loads:
        copy.start()
    sigma = sigma_ref[...]
    rate_row_ref[...] = (-0.5 * LOG2E) / (sigma * sigma)
    pack_catalog(sz, source_ref, edge_ref, member_ref, count_ref, pack_ref)
    loads.append(pltpu.make_async_copy(rate_row_ref, rate_ref, load_sem.at[2]))
    loads[-1].start()
    sent = pl.ds(0, sz.sent_rows)
    own = pltpu.make_async_copy(pack_ref.at[sent], cat_ref.at[zone, sent], own_cat)
    own.start()
    ends = lax.div(zone, zones - 1) + lax.div(zones - 1 - zone, zones - 1)
    pl.semaphore_wait(barrier, len(far) + len(near) + (bands - 1) * (2 - ends))
    copies = []
    for order, target in enumerate(far):
        copy = pltpu.make_async_remote_copy(
            src_ref=pack_ref.at[sent],
            dst_ref=cat_ref.at[zone, sent],
            send_sem=send_cat.at[order],
            recv_sem=recv_cat.at[order],
            device_id=target,
            device_id_type=MESH,
        )
        copy.start()
        copies.append(copy)
    for copy in loads:
        copy.wait()
    own.wait()
    for copy in copies:
        copy.wait()
    prepare(sz, cat_ref, stage_ref, turned_ref, col_ref, row_ref)

    def body(step, carry):
        tile_batch(
            sz, step, per, blob_ref, band_ref, shift_ref, amp_ref, rate_ref,
            pixel_ref, weight_ref, col_ref, row_ref, line_ref, result_ref,
        )
        return carry

    lax.fori_loop(0, sz.tiles // per, body, 0)
    route_terms(sz, blob_row_ref, result_ref, terms_ref)
    own = pltpu.make_async_copy(terms_ref.at[zone], got_ref.at[zone], own_term)
    own.start()
    copies = []
    for order, target in enumerate(far):
        copy = pltpu.make_async_remote_copy(
            src_ref=terms_ref.at[target[0]],
            dst_ref=got_ref.at[zone],
            send_sem=send_term.at[order],
            recv_sem=recv_term.at[order],
            device_id=target,
            device_id_type=MESH,
        )
        copy.start()
        copies.append(copy)
    find_seats(sz, zone, cat_ref, edge_ref, seat_ref)
    own.wait()
    for copy in copies:
        copy.wait()

    gather_terms(sz, got_ref, table_ref, part_ref)
    copies = []
    for order, target in enumerate(near):
        copy = pltpu.make_async_remote_copy(
            src_ref=part_ref.at[target[1]],
            dst_ref=sum_ref.at[order],
            send_sem=send_sum.at[order],
            recv_sem=recv_sum.at[order],
            device_id=target,
            device_id_type=MESH,
        )
        copy.start()
        copies.append(copy)
    for copy in copies:
        copy.wait()
    summed = part_ref[band]
    for order in range(len(near)):
        summed = summed + sum_ref[order]
    solved = solve(sz, summed, flat_ref, square_ref)
    eight = (HALF, LANES)
    packed = jnp.where(
        iota(eight, 1) < LANES // 2, solved[:HALF], pltpu.roll(solved[HALF:], LANES // 2, 1)
    )
    solved_ref[...] = packed
    flux_ref[bands + band] = packed

    def flux_copy(order, side, target):
        return pltpu.make_async_remote_copy(
            src_ref=solved_ref,
            dst_ref=flux_ref.at[side * bands + band],
            send_sem=send_flux.at[order],
            recv_sem=recv_flux.at[order],
            device_id=target,
            device_id_type=MESH,
        )

    across = []
    for number, (dz, sends, receives) in enumerate(beside):
        first = bands - 1 + number * bands
        group = [flux_copy(first + db, 1 - dz, at(dz, db)) for db in range(bands)]
        across.append((group, sends, receives))

        @pl.when(sends)
        def _():
            for copy in group:
                copy.start()

    copies = [flux_copy(order, 1, target) for order, target in enumerate(near)]
    for copy in copies:
        copy.start()
    for copy in copies:
        copy.wait()
    for group, sends, receives in across:

        @pl.when(sends)
        def _():
            for copy in group:
                copy.wait_send()

        @pl.when(receives)
        def _():
            for copy in group:
                copy.wait_recv()

    sub = iota(eight, 0)
    for part in range(sz.parts):
        span = slice(part * LANES, (part + 1) * LANES)
        slot = spread_rows(seat_ref[0:1, span], eight)
        blob = spread_rows(seat_ref[1:2, span], eight)
        row = slot % SLOTS
        key = slot // SLOTS * bands + blob // sz.share
        index = row // HALF * (LANES // 2) + blob % sz.share
        key = jnp.where(sub == row % HALF, key, -1)
        values = [jnp.zeros(eight, jnp.float32) for _ in range(FILTER_BANDS)]
        for table in range(3 * bands):
            flux = flux_ref[table]
            hit = key == table
            for k in range(FILTER_BANDS):
                values[k] = jnp.where(hit, take(flux, index + k * sz.share), values[k])
        out_ref[:, span] = jnp.concatenate(
            [jnp.sum(value, axis=0, keepdims=True) for value in values], axis=0
        )


def on_device(
    sizes, pixels, inv_var, tile_offset, psf_amp, psf_sigma, tile_blob, tile_band,
    source_pos, edge_rows, blob_members, sources_per_blob,
):
    zones, bands = sizes
    sz = Sizes(
        zones, bands, source_pos.shape[1], edge_rows.shape[0] // 2,
        sources_per_blob.shape[0], pixels.shape[0],
    )
    dma = pltpu.SemaphoreType.DMA
    f32 = jnp.float32
    tiles, height, width = pixels.shape
    per = TILES_STEP
    while tiles % per:
        per -= 1
    turned = -(-zones * HALF // LANES)
    near = 3 * bands - 1
    rows = sz.block + sz.third
    blob_row = tile_blob.reshape(1, -1)
    return pl.pallas_call(
        functools.partial(whole_kernel, sz, per),
        out_shape=jax.ShapeDtypeStruct((FILTER_BANDS, sz.sources), f32),
        in_specs=[ANY] * 2 + [SMEM] * 4 + [VMEM] * 6,
        out_specs=VMEM,
        scratch_shapes=[
            pltpu.VMEM((tiles, height, width), f32),
            pltpu.VMEM((tiles, height, width), f32),
            pltpu.VMEM((COMPS, tiles), f32),
            pltpu.SMEM((COMPS, tiles), f32),
            pltpu.VMEM((sz.cat_rows, LANES), f32),
            pltpu.VMEM((zones, sz.cat_rows, LANES), f32),
            pltpu.VMEM((turned * LANES, LANES), f32),
            pltpu.VMEM((turned, LANES, LANES), f32),
            pltpu.VMEM((zones, HALF, LANES), f32),
            pltpu.VMEM((zones * sz.blobs, LANES), f32),
            pltpu.VMEM((per, 3, height, width), f32),
            pltpu.VMEM((2, tiles, LANES), f32),
            pltpu.VMEM((zones, sz.rows, LANES), f32),
            pltpu.VMEM((zones, sz.rows, LANES), f32),
            pltpu.VMEM((sz.entries, 2 * LANES), f32),
            pltpu.VMEM((bands, rows, LANES), f32),
            pltpu.VMEM((bands - 1, rows, LANES), f32),
            pltpu.VMEM((LANES + 2 * SLOTS, LANES), f32),
            pltpu.VMEM((SLOTS, SLOTS, LANES), f32),
            pltpu.VMEM((HALF, LANES), f32),
            pltpu.VMEM((3 * bands, HALF, LANES), f32),
            pltpu.VMEM((8, sz.sources), jnp.int32),
            dma((3,)), dma((zones - 1,)), dma((zones - 1,)), dma,
            dma((zones - 1,)), dma((zones - 1,)), dma,
            dma((bands - 1,)), dma((bands - 1,)),
            dma((near,)), dma((near,)),
        ],
        compiler_params=pltpu.CompilerParams(
            collective_id=0, has_side_effects=True,
        ),
    )(
        pixels, inv_var, blob_row, tile_band.reshape(1, -1), tile_offset, psf_amp, psf_sigma,
        blob_row, source_pos, edge_rows.reshape(1, -1), blob_members.T,
        sources_per_blob.reshape(1, -1),
    )


def solution(mesh):
    sizes = (mesh.shape["zone"], mesh.shape["band"])
    return jax.shard_map(
        functools.partial(on_device, sizes),
        mesh=mesh,
        in_specs=(
            P(("zone", "band"), None, None),
            P(("zone", "band"), None, None),
            P(None, ("zone", "band")),
            P(None, ("zone", "band")),
            P(None, ("zone", "band")),
            P(("zone", "band")),
            P(("zone", "band")),
            P(None, "zone"),
            P("zone"),
            P("zone", None),
            P("zone"),
        ),
        out_specs=P(None, "zone"),
        check_vma=False,
    )
```

```python
import functools
import math

import jax
import jax.numpy as jnp
from jax import lax
from jax.experimental import pallas as pl
from jax.experimental.pallas import tpu as pltpu
from jax.sharding import PartitionSpec as P

FILTER_BANDS = 3
COMPS = 3
SLOTS = 16
HALF = SLOTS // 2
LANES = 128
SEATS = 4
SEAT = LANES // SEATS
TILES_STEP = 64
PRIOR = 1.0
FAR = 1.0e4
LOG2E = math.log2(math.e)

VMEM = pl.BlockSpec(memory_space=pltpu.VMEM)
SMEM = pl.BlockSpec(memory_space=pltpu.SMEM)
ANY = pl.BlockSpec(memory_space=pl.ANY)
MESH = pl.DeviceIdType.MESH


def iota(shape, axis):
    return lax.broadcasted_iota(jnp.int32, shape, axis)


def take(table, index):
    return jnp.take_along_axis(table, index, axis=1, mode="promise_in_bounds")


def spread_rows(row, shape):
    return jnp.broadcast_to(row, shape)


def lookup(rows, index):
    found = jnp.zeros(index.shape, rows[0].dtype)
    low = index & (LANES - 1)
    for part, row in enumerate(rows):
        hit = take(spread_rows(row, index.shape), low)
        found = jnp.where(index // LANES == part, hit, found)
    return found


def partner(zone, step, zones):
    if zones & (zones - 1):
        return lax.rem(zone + step, zones)
    other = 0
    bit = 1
    while bit < zones:
        digit = lax.rem(lax.div(zone, bit), 2)
        other = other + bit * ((1 - digit) if step & bit else digit)
        bit *= 2
    return other


class Sizes:
    def __init__(self, zones, bands, sources, edge, blobs, tiles):
        self.zones, self.bands = zones, bands
        self.sources, self.edge, self.blobs, self.tiles = sources, edge, blobs, tiles
        self.parts = sources // LANES
        self.member_row = -(-2 * self.parts // 8) * 8
        self.edge_row = self.member_row + HALF
        self.cat_rows = self.edge_row + 8
        self.sent_rows = self.edge_row + 2
        capacity = max(SEATS, (2 * tiles + zones - 1) // zones)
        self.capacity = -(-capacity // SEATS) * SEATS
        self.rest = self.capacity // SEATS
        self.rows = -(-(self.capacity + self.rest) // 8) * 8
        self.share = blobs // bands
        self.systems = FILTER_BANDS * self.share
        self.block = -(-self.systems // 8) * 8
        self.third = self.block // FILTER_BANDS
        self.entries = zones * self.capacity


def pack_catalog(sz, source_ref, edge_ref, member_ref, count_ref, pack_ref):
    shape = (8, LANES)
    edges = spread_rows(edge_ref[...], shape)
    for coord in range(2):
        rows = []
        for part in range(sz.parts):
            row = source_ref[coord : coord + 1, part * LANES : (part + 1) * LANES]
            pack_ref[coord * sz.parts + part : coord * sz.parts + part + 1, :] = row
            rows.append(row)
        at = sz.edge_row + coord
        pack_ref[at : at + 1, :] = lookup(rows, edges)[:1]
    slot = iota((SLOTS, sz.blobs), 0)
    member = jnp.where(slot < count_ref[...], member_ref[...], -1).astype(jnp.float32)
    pack_ref[sz.member_row : sz.member_row + HALF, :] = jnp.concatenate(
        [member[:HALF], member[HALF:]], axis=1
    )


def resolve_zone(sz, zone, cat_ref, stage_ref, col_ref):
    shape = (HALF, LANES)
    member = cat_ref[zone, sz.member_row : sz.member_row + HALF, :].astype(jnp.int32)
    if isinstance(zone, int):
        before, after = max(zone - 1, 0), min(zone + 1, sz.zones - 1)
    else:
        before, after = jnp.maximum(zone - 1, 0), jnp.minimum(zone + 1, sz.zones - 1)
    low = member < sz.edge
    high = member >= sz.edge + sz.sources
    own = jnp.clip(member - sz.edge, 0, sz.sources - 1)
    rim = jnp.where(
        low, sz.edge + jnp.maximum(member, 0), jnp.where(high, member - sz.edge - sz.sources, 0)
    )
    lane = iota(shape, 1)
    for coord in range(2):
        rows = [
            cat_ref[zone, coord * sz.parts + part : coord * sz.parts + part + 1, :]
            for part in range(sz.parts)
        ]
        at = sz.edge_row + coord
        table = jnp.where(
            lane >= sz.edge,
            spread_rows(cat_ref[before, at : at + 1, :], shape),
            spread_rows(cat_ref[after, at : at + 1, :], shape),
        )
        place = jnp.where(low | high, take(table, rim), lookup(rows, own))
        if coord == 0:
            place = jnp.where(member < 0, FAR, place)
            start = zone * HALF if isinstance(zone, int) else pl.multiple_of(zone * HALF, HALF)
            stage_ref[pl.ds(start, HALF), :] = place
        else:
            col_ref[zone] = place


def spread_zone(sz, zone, turned_ref, row_ref):
    shape = (8, LANES)
    lane = iota(shape, 1)
    per = LANES // HALF
    index = (zone % per) * HALF + lane % HALF
    upper = lane % SLOTS >= HALF
    for part in range(sz.blobs // 8):
        pieces = []
        for half in range(2):
            at = half * sz.blobs + part * 8
            pieces.append(take(turned_ref[zone // per, at : at + 8, :], index))
        start = zone * sz.blobs + part * 8
        if not isinstance(zone, int):
            start = pl.multiple_of(start, 8)
        row_ref[pl.ds(start, 8), :] = jnp.where(upper, pieces[1], pieces[0])


def prepare(sz, cat_ref, stage_ref, turned_ref, col_ref, row_ref):
    each = (lambda body: [body(z) for z in range(sz.zones)]) if sz.zones <= 8 else (
        lambda body: lax.fori_loop(0, sz.zones, lambda z, c: (body(z), c)[1], 0)
    )
    each(lambda z: resolve_zone(sz, z, cat_ref, stage_ref, col_ref))
    for part in range(turned_ref.shape[0]):
        turned_ref[part] = stage_ref[part * LANES : (part + 1) * LANES, :].T
    each(lambda z: spread_zone(sz, z, turned_ref, row_ref))


def split(value):
    head = value.astype(jnp.bfloat16)
    return head, (value - head.astype(jnp.float32)).astype(jnp.bfloat16)


def tile_batch(
    sz, step, per, blob_ref, band_ref, shift_ref, amp_ref, rate_ref, pixel_ref, weight_ref,
    col_ref, row_ref, line_ref, result_ref,
):
    height = pixel_ref.shape[1]
    eight = (HALF, LANES)
    shape = (SLOTS, LANES)
    lane = iota(eight, 1)
    sub = iota(eight, 0)
    sub_f = sub.astype(jnp.float32)
    lane_f = lane.astype(jnp.float32)
    slots_all = COMPS * SLOTS
    width = COMPS * HALF
    keep = (iota(shape, 1) % HALF == iota(shape, 0) % HALF) & (iota(shape, 1) < 3 * width)
    keep = jnp.where(keep, 1.0, 0.0).astype(jnp.bfloat16)
    comp = lane // SLOTS % COMPS
    high_part = (lane < width) | (lane >= 2 * width)
    half_index = lane // HALF % COMPS * SLOTS + lane % HALF
    seat_a = lane // HALF == sub
    seat_b = lane // HALF == sub + HALF
    blank = jnp.zeros((LANES - 3 * width, LANES), jnp.float32)
    zero_tail = jnp.zeros((slots_all, LANES), jnp.bfloat16)
    zero_rows = jnp.zeros((LANES - 2 * slots_all, LANES), jnp.bfloat16)
    pending = []

    for slot in range(per):
        tile = step * per + slot
        blob = blob_ref[0, tile]
        zone = lax.div(blob, sz.blobs)
        local = lax.rem(blob, sz.blobs)
        rate = [rate_ref[g, tile] for g in range(COMPS)]
        amp = [amp_ref[g, tile] for g in range(COMPS)]
        row_rate = jnp.where(comp == 0, rate[0], jnp.where(comp == 1, rate[1], rate[2]))
        row_amp = jnp.where(comp == 0, amp[0], jnp.where(comp == 1, amp[1], amp[2]))
        row_shift = shift_ref[0, tile]
        row_base = row_shift + spread_rows(row_ref[pl.ds(blob, 1), :], eight)
        col_base = shift_ref[1, tile]
        col_table = col_ref[zone]
        square = []
        for half in range(2):
            index = jnp.full(eight, half * sz.blobs, jnp.int32) + local
            away = lane_f - col_base - take(col_table, index)
            square.append(away * away)
        cols = [[jnp.exp2(rate[g] * square[half]) for half in range(2)] for g in range(COMPS)]
        heads, tails, heads_f, tails_f = [], [], [], []
        for g in range(COMPS):
            both = jnp.concatenate(cols[g], axis=0)
            head = both.astype(jnp.bfloat16)
            head_f = head.astype(jnp.float32)
            heads.append(head)
            heads_f.append(head_f)
            tails_f.append(both - head_f)
            tails.append(tails_f[-1].astype(jnp.bfloat16))
        rights = []
        for half in range(2):
            span = slice(half * HALF, (half + 1) * HALF)
            top = [h[span] for h in heads_f]
            rights.append(
                jnp.concatenate(top + top + [t[span] for t in tails_f] + [blank], axis=0).astype(
                    jnp.bfloat16
                )
            )
        rows = []
        for part in range(height // 8):
            away = (sub_f + 8.0 * part) - row_base
            value = jnp.exp2(row_rate * (away * away)) * row_amp
            rows.append(value)
            line_ref[slot, 0, part * 8 : (part + 1) * 8, :] = value
            for half in range(2):
                seen = take(value, half_index + half * HALF)
                head = seen.astype(jnp.bfloat16).astype(jnp.float32)
                line_ref[slot, 1 + half, part * 8 : (part + 1) * 8, :] = jnp.where(
                    high_part, head, seen - head
                )
        models = []
        for half in range(2):
            left = []
            for i in range(0, height, 2):
                pair = jnp.concatenate(
                    [
                        spread_rows(line_ref[slot, 1 + half, i + d : i + d + 1, :], eight)
                        for d in range(2)
                    ],
                    axis=0,
                )
                left.append(pair.astype(jnp.bfloat16) * keep)
            models.append(
                lax.dot_general(
                    jnp.concatenate(left, axis=0), rights[half], (((1,), (0,)), ((), ())),
                    preferred_element_type=jnp.float32,
                )
            )
        heads_left = []
        tails_left = []
        for i in range(height):
            span = slice(i * HALF, (i + 1) * HALF)
            weight = spread_rows(weight_ref[tile, i : i + 1, :], shape)
            scaled = jnp.concatenate([models[0][span], models[1][span]], axis=0) * weight
            head, tail = split(scaled)
            heads_left.append(head)
            tails_left.append(tail)
        head, tail = split(weight_ref[tile] * pixel_ref[tile])
        heads_left.append(head)
        tails_left.append(tail)
        top = jnp.concatenate(heads, axis=0)
        low = jnp.concatenate(tails, axis=0)
        pending.append((tile, blob, local, slot, rows, heads_left, tails_left, top, low))
        if len(pending) < 2:
            continue
        left = [
            jnp.concatenate([pending[0][5][i], pending[1][5][i], pending[0][6][i], pending[1][6][i]], axis=1)
            for i in range(height + 1)
        ]
        zero = zero_tail
        right = jnp.concatenate(
            [
                jnp.concatenate([pending[0][7], zero, pending[0][7], zero], axis=1),
                jnp.concatenate([pending[0][8], zero, zero, zero], axis=1),
                jnp.concatenate([zero_rows] * 4, axis=1),
                jnp.concatenate([zero, pending[1][7], zero, pending[1][7]], axis=1),
                jnp.concatenate([zero, pending[1][8], zero, zero], axis=1),
                jnp.concatenate([zero_rows] * 4, axis=1),
            ],
            axis=0,
        )
        product = lax.dot_general(
            jnp.concatenate(left, axis=0), right, (((1,), (1,)), ((), ())),
            preferred_element_type=jnp.float32,
        )
        for member in range(2):
            tile, blob, local, held, rows = pending[member][:5]
            side = slice(member * LANES, (member + 1) * LANES)
            normal = None
            for i in range(height):
                line = spread_rows(line_ref[held, 0, i : i + 1, :], shape)
                term = product[i * SLOTS : (i + 1) * SLOTS, side] * line
                normal = term if normal is None else normal + term
            vector = None
            for part in range(height // 8):
                at = height * SLOTS + part * 8
                term = product[at : at + 8, side] * rows[part]
                vector = term if vector is None else vector + term
            folded = jnp.concatenate([normal, vector], axis=0)
            for shift in (LANES // 2, LANES // 4, LANES // 8):
                folded = folded + pltpu.roll(folded, shift, 1)
            upper, lower, vector = folded[:HALF], folded[HALF:SLOTS], folded[SLOTS:]
            step_back = SLOTS - HALF - 1
            main = jnp.where(
                seat_a, pltpu.roll(upper, 0, 1, stride=step_back, stride_axis=0),
                jnp.where(
                    seat_b,
                    pltpu.roll(lower, HALF * step_back, 1, stride=step_back, stride_axis=0), 0.0,
                ),
            )
            code = (
                lax.div(local, sz.share) * sz.systems
                + band_ref[0, tile] * sz.share
                + lax.rem(local, sz.share)
            )
            rest = jnp.where(lane == sub, pltpu.roll(upper, HALF, 1), 0.0)
            rest = jnp.where((lane >= SLOTS) & (lane < 2 * SLOTS), vector, rest)
            rest = jnp.where((lane == HALF) & (sub == 0), code.astype(jnp.float32), rest)
            result_ref[0, pl.ds(tile, 1), :] = jnp.sum(main, axis=0, keepdims=True)
            result_ref[1, pl.ds(tile, 1), :] = jnp.sum(rest, axis=0, keepdims=True)
        pending = []


def route_terms(sz, blob_ref, result_ref, terms_ref):
    square = (sz.tiles, sz.tiles)
    zone = spread_rows(lax.div(blob_ref[...], sz.blobs).astype(jnp.float32), square)
    same = (zone == zone.T) & (iota(square, 0) < iota(square, 1))
    rank = jnp.sum(jnp.where(same, 1.0, 0.0), axis=0, keepdims=True)
    place = zone[:1] * float(sz.capacity) + rank
    entry = iota((sz.entries, sz.tiles), 0).astype(jnp.float32)
    hit = jnp.where(entry == place, 1.0, 0.0).astype(jnp.bfloat16)
    left = jnp.concatenate([result_ref[0], result_ref[1]], axis=1)
    moved = None
    for _ in range(3):
        piece = left.astype(jnp.bfloat16)
        left = left - piece.astype(jnp.float32)
        part = lax.dot_general(
            hit, piece, (((1,), (0,)), ((), ())), preferred_element_type=jnp.float32
        )
        moved = part if moved is None else moved + part
    for number in range(sz.zones):
        start = number * sz.capacity
        terms_ref[number, : sz.capacity, :] = moved[start : start + sz.capacity, :LANES]
        total = None
        for seat in range(SEATS):
            at = start + seat * sz.rest
            piece = moved[at : at + sz.rest, LANES:]
            piece = pltpu.roll(piece, seat * SEAT, 1) if seat else piece
            total = piece if total is None else total + piece
        terms_ref[number, sz.capacity : sz.capacity + sz.rest, :] = total


def find_seats(sz, zone, cat_ref, edge_ref, seat_ref):
    shape = (HALF, LANES)
    edges = spread_rows(edge_ref[...], shape)
    source = iota((sz.sources, LANES), 0)
    lane = iota((1, LANES), 1)
    total = None
    for side in range(3):
        near = lax.rem(zone + side - 1 + sz.zones, sz.zones)
        member = cat_ref[near, sz.member_row : sz.member_row + HALF, :].astype(jnp.int32)
        top = sz.edge + sz.sources
        if side == 0:
            valid = (member >= top) & (zone > 0)
            target = take(edges, jnp.where(valid, member - top, 0))
        elif side == 1:
            valid = (member >= sz.edge) & (member < top)
            target = member - sz.edge
        else:
            valid = (member >= 0) & (member < sz.edge) & (zone < sz.zones - 1)
            target = take(edges, jnp.where(valid, member + sz.edge, 0))
        target = jnp.where(valid, target, -1)
        for row in range(HALF):
            hit = source == target[row : row + 1, :]
            right = jnp.where(hit, 1.0, 0.0).astype(jnp.bfloat16)
            slot = side * SLOTS + row + lane // sz.blobs * HALF
            left = jnp.concatenate(
                [slot, lane % sz.blobs, jnp.zeros((SLOTS - 2, LANES), jnp.int32)], axis=0
            )
            part = lax.dot_general(
                left.astype(jnp.float32).astype(jnp.bfloat16), right, (((1,), (1,)), ((), ())),
                preferred_element_type=jnp.float32,
            )
            total = part if total is None else total + part
    seat_ref[...] = total[:8].astype(jnp.int32)


def gather_terms(sz, got_ref, table_ref, part_ref):
    for zone in range(sz.zones):
        start = zone * sz.capacity
        table_ref[start : start + sz.capacity, :LANES] = got_ref[zone, : sz.capacity, :]
        rest = got_ref[zone, sz.capacity : sz.capacity + sz.rest, :]
        for seat in range(SEATS):
            at = start + seat * sz.rest
            table_ref[at : at + sz.rest, LANES:] = (
                pltpu.roll(rest, LANES - seat * SEAT, 1) if seat else rest
            )
    square = (LANES, LANES)
    diagonal = iota(square, 0) == iota(square, 1)
    codes = []
    for at in range(0, sz.entries, LANES):
        block = table_ref[at : at + LANES, LANES:]
        code = take(block, jnp.full(square, HALF, jnp.int32))
        codes.append(jnp.sum(jnp.where(diagonal, code, 0.0), axis=0, keepdims=True))
    codes = jnp.concatenate(codes, axis=1)
    count = sz.bands * sz.block
    system = iota((count, sz.entries), 0)
    hit = jnp.where(system.astype(jnp.float32) == codes, 1.0, 0.0).astype(jnp.bfloat16)
    head, tail = split(table_ref[...])
    dims = (((1,), (0,)), ((), ()))
    total = lax.dot_general(hit, head, dims, preferred_element_type=jnp.float32)
    total = total + lax.dot_general(hit, tail, dims, preferred_element_type=jnp.float32)
    lane = iota((sz.third, LANES), 1) // SEAT
    for owner in range(sz.bands):
        start = owner * sz.block
        part_ref[owner, : sz.block, :] = total[start : start + sz.block, :LANES]
        rest = None
        for seat in range(FILTER_BANDS):
            at = start + seat * sz.third
            piece = total[at : at + sz.third, LANES:]
            piece = jnp.where(lane == seat, pltpu.roll(piece, seat * SEAT, 1) if seat else piece, 0.0)
            rest = piece if rest is None else rest + piece
        part_ref[owner, sz.block :, :] = rest


def solve(sz, summed, flat_ref, square_ref):
    main, rest = summed[: sz.block], summed[sz.block :]
    rest = jnp.concatenate(
        [pltpu.roll(rest, LANES - s * SEAT, 1) if s else rest for s in range(FILTER_BANDS)], axis=0
    )
    fill = jnp.zeros((LANES - sz.block, LANES), jnp.float32)
    flat_ref[:LANES, :] = jnp.concatenate([main, fill], axis=0).T
    flat_ref[LANES:, :] = jnp.concatenate([rest, fill], axis=0).T[: 2 * SLOTS]
    for l in range(SLOTS):
        for j in range(SLOTS):
            away = (l - j) % SLOTS
            if away < HALF:
                at = HALF * j + away
            elif away == HALF:
                at = LANES + min(j, l)
            else:
                at = HALF * l + SLOTS - away
            square_ref[l, j : j + 1, :] = flat_ref[at : at + 1, :]
    shape = (SLOTS, LANES)
    sub = iota(shape, 0)
    columns = [square_ref[l] + jnp.where(sub == l, PRIOR, 0.0) for l in range(SLOTS)]
    columns.append(flat_ref[LANES + SLOTS : LANES + 2 * SLOTS, :])
    scale = columns[0]
    for k in range(SLOTS):
        column = columns[k]
        inverse = 1.0 / column[k : k + 1]
        scale = jnp.where(sub == k, column, scale)
        column = jnp.where(sub == k, 0.0, column)
        for l in range(k + 1, SLOTS + 1):
            ratio = columns[l][k : k + 1] * inverse
            columns[l] = columns[l] - column * ratio
    return columns[SLOTS] / scale


def whole_kernel(
    sz, per,
    pixel_hbm, weight_hbm, blob_hbm, band_hbm, shift_hbm, amp_hbm, sigma_hbm,
    source_hbm, edge_hbm, member_hbm, count_hbm, out_ref,
    blob_ref, band_ref, shift_ref, amp_ref, sigma_ref, blob_row_ref,
    source_ref, edge_ref, member_ref, count_ref, pixel_ref, weight_ref, rate_row_ref, rate_ref, pack_ref, cat_ref,
    stage_ref, turned_ref, col_ref, row_ref, line_ref, result_ref, terms_ref,
    got_ref, table_ref, part_ref, sum_ref, flat_ref, square_ref, solved_ref, flux_ref, seat_ref,
    load_sem, send_cat, recv_cat, own_cat,
    send_term, recv_term, own_term, send_sum, recv_sum, send_flux, recv_flux,
):
    zones, bands = sz.zones, sz.bands
    zone = lax.axis_index("zone")
    band = lax.axis_index("band")
    at = lambda dz, db: (lax.rem(zone + dz + zones, zones), lax.rem(band + db, bands))
    far = [(partner(zone, step, zones), band) for step in range(zones - 1, 0, -1)]
    near = [at(0, db) for db in range(1, bands)]
    above, below = zone < zones - 1, zone > 0
    beside = [(1, above, below), (-1, below, above)]
    barrier = pltpu.get_barrier_semaphore()

    def greet(target):
        pl.semaphore_signal(barrier, inc=1, device_id=target, device_id_type=MESH)

    for target in far + near:
        greet(target)
    for dz, sends, _ in beside:

        @pl.when(sends)
        def _():
            for db in range(1, bands):
                greet(at(dz, db))

    pairs = [
        (source_hbm, source_ref), (edge_hbm, edge_ref), (member_hbm, member_ref),
        (count_hbm, count_ref), (sigma_hbm, sigma_ref), (blob_hbm, blob_ref),
        (blob_hbm, blob_row_ref), (band_hbm, band_ref), (shift_hbm, shift_ref),
        (amp_hbm, amp_ref), (pixel_hbm, pixel_ref), (weight_hbm, weight_ref),
    ]
    loads = [
        pltpu.make_async_copy(source, target, load_sem.at[number])
        for number, (source, target) in enumerate(pairs)
    ]
    for copy in loads:
        copy.start()
    for copy in loads[:5]:
        copy.wait()
    loads = loads[5:]
    sigma = sigma_ref[...]
    rate_row_ref[...] = (-0.5 * LOG2E) / (sigma * sigma)
    pack_catalog(sz, source_ref, edge_ref, member_ref, count_ref, pack_ref)
    loads.append(pltpu.make_async_copy(rate_row_ref, rate_ref, load_sem.at[len(pairs)]))
    loads[-1].start()
    sent = pl.ds(0, sz.sent_rows)
    own = pltpu.make_async_copy(pack_ref.at[sent], cat_ref.at[zone, sent], own_cat)
    own.start()
    ends = lax.div(zone, zones - 1) + lax.div(zones - 1 - zone, zones - 1)
    pl.semaphore_wait(barrier, len(far) + len(near) + (bands - 1) * (2 - ends))
    copies = []
    for order, target in enumerate(far):
        copy = pltpu.make_async_remote_copy(
            src_ref=pack_ref.at[sent],
            dst_ref=cat_ref.at[zone, sent],
            send_sem=send_cat.at[order],
            recv_sem=recv_cat.at[order],
            device_id=target,
            device_id_type=MESH,
        )
        copy.start()
        copies.append(copy)
    for copy in loads:
        copy.wait()
    own.wait()
    for copy in copies:
        copy.wait()
    prepare(sz, cat_ref, stage_ref, turned_ref, col_ref, row_ref)

    def body(step, carry):
        tile_batch(
            sz, step, per, blob_ref, band_ref, shift_ref, amp_ref, rate_ref,
            pixel_ref, weight_ref, col_ref, row_ref, line_ref, result_ref,
        )
        return carry

    lax.fori_loop(0, sz.tiles // per, body, 0)
    route_terms(sz, blob_row_ref, result_ref, terms_ref)
    own = pltpu.make_async_copy(terms_ref.at[zone], got_ref.at[zone], own_term)
    own.start()
    copies = []
    for order, target in enumerate(far):
        copy = pltpu.make_async_remote_copy(
            src_ref=terms_ref.at[target[0]],
            dst_ref=got_ref.at[zone],
            send_sem=send_term.at[order],
            recv_sem=recv_term.at[order],
            device_id=target,
            device_id_type=MESH,
        )
        copy.start()
        copies.append(copy)
    find_seats(sz, zone, cat_ref, edge_ref, seat_ref)
    own.wait()
    for copy in copies:
        copy.wait()

    gather_terms(sz, got_ref, table_ref, part_ref)
    copies = []
    for order, target in enumerate(near):
        copy = pltpu.make_async_remote_copy(
            src_ref=part_ref.at[target[1]],
            dst_ref=sum_ref.at[order],
            send_sem=send_sum.at[order],
            recv_sem=recv_sum.at[order],
            device_id=target,
            device_id_type=MESH,
        )
        copy.start()
        copies.append(copy)
    for copy in copies:
        copy.wait()
    summed = part_ref[band]
    for order in range(len(near)):
        summed = summed + sum_ref[order]
    solved = solve(sz, summed, flat_ref, square_ref)
    eight = (HALF, LANES)
    packed = jnp.where(
        iota(eight, 1) < LANES // 2, solved[:HALF], pltpu.roll(solved[HALF:], LANES // 2, 1)
    )
    solved_ref[...] = packed
    flux_ref[bands + band] = packed

    def flux_copy(order, side, target):
        return pltpu.make_async_remote_copy(
            src_ref=solved_ref,
            dst_ref=flux_ref.at[side * bands + band],
            send_sem=send_flux.at[order],
            recv_sem=recv_flux.at[order],
            device_id=target,
            device_id_type=MESH,
        )

    across = []
    for number, (dz, sends, receives) in enumerate(beside):
        first = bands - 1 + number * bands
        group = [flux_copy(first + db, 1 - dz, at(dz, db)) for db in range(bands)]
        across.append((group, sends, receives))

        @pl.when(sends)
        def _():
            for copy in group:
                copy.start()

    copies = [flux_copy(order, 1, target) for order, target in enumerate(near)]
    for copy in copies:
        copy.start()
    for copy in copies:
        copy.wait()
    for group, sends, receives in across:

        @pl.when(sends)
        def _():
            for copy in group:
                copy.wait_send()

        @pl.when(receives)
        def _():
            for copy in group:
                copy.wait_recv()

    sub = iota(eight, 0)
    for part in range(sz.parts):
        span = slice(part * LANES, (part + 1) * LANES)
        slot = spread_rows(seat_ref[0:1, span], eight)
        blob = spread_rows(seat_ref[1:2, span], eight)
        row = slot % SLOTS
        key = slot // SLOTS * bands + blob // sz.share
        index = row // HALF * (LANES // 2) + blob % sz.share
        key = jnp.where(sub == row % HALF, key, -1)
        values = [jnp.zeros(eight, jnp.float32) for _ in range(FILTER_BANDS)]
        for table in range(3 * bands):
            flux = flux_ref[table]
            hit = key == table
            for k in range(FILTER_BANDS):
                values[k] = jnp.where(hit, take(flux, index + k * sz.share), values[k])
        out_ref[:, span] = jnp.concatenate(
            [jnp.sum(value, axis=0, keepdims=True) for value in values], axis=0
        )


def on_device(
    sizes, pixels, inv_var, tile_offset, psf_amp, psf_sigma, tile_blob, tile_band,
    source_pos, edge_rows, blob_members, sources_per_blob,
):
    zones, bands = sizes
    sz = Sizes(
        zones, bands, source_pos.shape[1], edge_rows.shape[0] // 2,
        sources_per_blob.shape[0], pixels.shape[0],
    )
    dma = pltpu.SemaphoreType.DMA
    f32 = jnp.float32
    tiles, height, width = pixels.shape
    per = TILES_STEP
    while tiles % per:
        per -= 1
    turned = -(-zones * HALF // LANES)
    near = 3 * bands - 1
    rows = sz.block + sz.third
    blob_row = tile_blob.reshape(1, -1)
    return pl.pallas_call(
        functools.partial(whole_kernel, sz, per),
        out_shape=jax.ShapeDtypeStruct((FILTER_BANDS, sz.sources), f32),
        in_specs=[ANY] * 11,
        out_specs=VMEM,
        scratch_shapes=[
            pltpu.SMEM((1, tiles), jnp.int32),
            pltpu.SMEM((1, tiles), jnp.int32),
            pltpu.SMEM((2, tiles), f32),
            pltpu.SMEM((COMPS, tiles), f32),
            pltpu.VMEM((COMPS, tiles), f32),
            pltpu.VMEM((1, tiles), jnp.int32),
            pltpu.VMEM((2, sz.sources), f32),
            pltpu.VMEM((1, 2 * sz.edge), jnp.int32),
            pltpu.VMEM((SLOTS, sz.blobs), jnp.int32),
            pltpu.VMEM((1, sz.blobs), jnp.int32),
            pltpu.VMEM((tiles, height, width), f32),
            pltpu.VMEM((tiles, height, width), f32),
            pltpu.VMEM((COMPS, tiles), f32),
            pltpu.SMEM((COMPS, tiles), f32),
            pltpu.VMEM((sz.cat_rows, LANES), f32),
            pltpu.VMEM((zones, sz.cat_rows, LANES), f32),
            pltpu.VMEM((turned * LANES, LANES), f32),
            pltpu.VMEM((turned, LANES, LANES), f32),
            pltpu.VMEM((zones, HALF, LANES), f32),
            pltpu.VMEM((zones * sz.blobs, LANES), f32),
            pltpu.VMEM((per, 3, height, width), f32),
            pltpu.VMEM((2, tiles, LANES), f32),
            pltpu.VMEM((zones, sz.rows, LANES), f32),
            pltpu.VMEM((zones, sz.rows, LANES), f32),
            pltpu.VMEM((sz.entries, 2 * LANES), f32),
            pltpu.VMEM((bands, rows, LANES), f32),
            pltpu.VMEM((bands - 1, rows, LANES), f32),
            pltpu.VMEM((LANES + 2 * SLOTS, LANES), f32),
            pltpu.VMEM((SLOTS, SLOTS, LANES), f32),
            pltpu.VMEM((HALF, LANES), f32),
            pltpu.VMEM((3 * bands, HALF, LANES), f32),
            pltpu.VMEM((8, sz.sources), jnp.int32),
            dma((13,)), dma((zones - 1,)), dma((zones - 1,)), dma,
            dma((zones - 1,)), dma((zones - 1,)), dma,
            dma((bands - 1,)), dma((bands - 1,)),
            dma((near,)), dma((near,)),
        ],
        compiler_params=pltpu.CompilerParams(
            collective_id=0, has_side_effects=True,
        ),
    )(
        pixels, inv_var, blob_row, tile_band.reshape(1, -1), tile_offset, psf_amp, psf_sigma,
        source_pos, edge_rows.reshape(1, -1), blob_members.T,
        sources_per_blob.reshape(1, -1),
    )


def solution(mesh):
    sizes = (mesh.shape["zone"], mesh.shape["band"])
    return jax.shard_map(
        functools.partial(on_device, sizes),
        mesh=mesh,
        in_specs=(
            P(("zone", "band"), None, None),
            P(("zone", "band"), None, None),
            P(None, ("zone", "band")),
            P(None, ("zone", "band")),
            P(None, ("zone", "band")),
            P(("zone", "band")),
            P(("zone", "band")),
            P(None, "zone"),
            P("zone"),
            P("zone", None),
            P("zone"),
        ),
        out_specs=P(None, "zone"),
        check_vma=False,
    )
```

```python
import functools
import math

import jax
import jax.numpy as jnp
from jax import lax
from jax.experimental import pallas as pl
from jax.experimental.pallas import tpu as pltpu
from jax.sharding import PartitionSpec as P

FILTER_BANDS = 3
COMPS = 3
SLOTS = 16
HALF = SLOTS // 2
LANES = 128
SEATS = 4
SEAT = LANES // SEATS
TILES_STEP = 64
PRIOR = 1.0
FAR = 1.0e4
LOG2E = math.log2(math.e)

VMEM = pl.BlockSpec(memory_space=pltpu.VMEM)
SMEM = pl.BlockSpec(memory_space=pltpu.SMEM)
ANY = pl.BlockSpec(memory_space=pl.ANY)
MESH = pl.DeviceIdType.MESH


def iota(shape, axis):
    return lax.broadcasted_iota(jnp.int32, shape, axis)


def take(table, index):
    return jnp.take_along_axis(table, index, axis=1, mode="promise_in_bounds")


def spread_rows(row, shape):
    return jnp.broadcast_to(row, shape)


def lookup(rows, index):
    found = jnp.zeros(index.shape, rows[0].dtype)
    low = index & (LANES - 1)
    for part, row in enumerate(rows):
        hit = take(spread_rows(row, index.shape), low)
        found = jnp.where(index // LANES == part, hit, found)
    return found


def partner(zone, step, zones):
    if zones & (zones - 1):
        return lax.rem(zone + step, zones)
    other = 0
    bit = 1
    while bit < zones:
        digit = lax.rem(lax.div(zone, bit), 2)
        other = other + bit * ((1 - digit) if step & bit else digit)
        bit *= 2
    return other


class Sizes:
    def __init__(self, zones, bands, sources, edge, blobs, tiles):
        self.zones, self.bands = zones, bands
        self.sources, self.edge, self.blobs, self.tiles = sources, edge, blobs, tiles
        self.parts = sources // LANES
        self.member_row = -(-2 * self.parts // 8) * 8
        self.edge_row = self.member_row + HALF
        self.cat_rows = self.edge_row + 8
        self.sent_rows = self.edge_row + 2
        capacity = max(SEATS, (2 * tiles + zones - 1) // zones)
        self.capacity = -(-capacity // SEATS) * SEATS
        self.rest = self.capacity // SEATS
        self.rows = -(-(self.capacity + self.rest) // 8) * 8
        self.share = blobs // bands
        self.systems = FILTER_BANDS * self.share
        self.block = -(-self.systems // 8) * 8
        self.third = self.block // FILTER_BANDS
        self.entries = zones * self.capacity


def pack_catalog(sz, source_ref, edge_ref, member_ref, count_ref, pack_ref):
    shape = (8, LANES)
    edges = spread_rows(edge_ref[...], shape)
    for coord in range(2):
        rows = []
        for part in range(sz.parts):
            row = source_ref[coord : coord + 1, part * LANES : (part + 1) * LANES]
            pack_ref[coord * sz.parts + part : coord * sz.parts + part + 1, :] = row
            rows.append(row)
        at = sz.edge_row + coord
        pack_ref[at : at + 1, :] = lookup(rows, edges)[:1]
    slot = iota((SLOTS, sz.blobs), 0)
    member = jnp.where(slot < count_ref[...], member_ref[...], -1).astype(jnp.float32)
    pack_ref[sz.member_row : sz.member_row + HALF, :] = jnp.concatenate(
        [member[:HALF], member[HALF:]], axis=1
    )


def resolve_zone(sz, zone, cat_ref, stage_ref, col_ref):
    shape = (HALF, LANES)
    member = cat_ref[zone, sz.member_row : sz.member_row + HALF, :].astype(jnp.int32)
    if isinstance(zone, int):
        before, after = max(zone - 1, 0), min(zone + 1, sz.zones - 1)
    else:
        before, after = jnp.maximum(zone - 1, 0), jnp.minimum(zone + 1, sz.zones - 1)
    low = member < sz.edge
    high = member >= sz.edge + sz.sources
    own = jnp.clip(member - sz.edge, 0, sz.sources - 1)
    rim = jnp.where(
        low, sz.edge + jnp.maximum(member, 0), jnp.where(high, member - sz.edge - sz.sources, 0)
    )
    lane = iota(shape, 1)
    for coord in range(2):
        rows = [
            cat_ref[zone, coord * sz.parts + part : coord * sz.parts + part + 1, :]
            for part in range(sz.parts)
        ]
        at = sz.edge_row + coord
        table = jnp.where(
            lane >= sz.edge,
            spread_rows(cat_ref[before, at : at + 1, :], shape),
            spread_rows(cat_ref[after, at : at + 1, :], shape),
        )
        place = jnp.where(low | high, take(table, rim), lookup(rows, own))
        if coord == 0:
            place = jnp.where(member < 0, FAR, place)
            start = zone * HALF if isinstance(zone, int) else pl.multiple_of(zone * HALF, HALF)
            stage_ref[pl.ds(start, HALF), :] = place
        else:
            col_ref[zone] = place


def spread_zone(sz, zone, turned_ref, row_ref):
    shape = (8, LANES)
    lane = iota(shape, 1)
    per = LANES // HALF
    index = (zone % per) * HALF + lane % HALF
    upper = lane % SLOTS >= HALF
    for part in range(sz.blobs // 8):
        pieces = []
        for half in range(2):
            at = half * sz.blobs + part * 8
            pieces.append(take(turned_ref[zone // per, at : at + 8, :], index))
        start = zone * sz.blobs + part * 8
        if not isinstance(zone, int):
            start = pl.multiple_of(start, 8)
        row_ref[pl.ds(start, 8), :] = jnp.where(upper, pieces[1], pieces[0])


def prepare(sz, cat_ref, stage_ref, turned_ref, col_ref, row_ref):
    each = (lambda body: [body(z) for z in range(sz.zones)]) if sz.zones <= 8 else (
        lambda body: lax.fori_loop(0, sz.zones, lambda z, c: (body(z), c)[1], 0)
    )
    each(lambda z: resolve_zone(sz, z, cat_ref, stage_ref, col_ref))
    for part in range(turned_ref.shape[0]):
        turned_ref[part] = stage_ref[part * LANES : (part + 1) * LANES, :].T
    each(lambda z: spread_zone(sz, z, turned_ref, row_ref))


def split(value):
    head = value.astype(jnp.bfloat16)
    return head, (value - head.astype(jnp.float32)).astype(jnp.bfloat16)


def tile_batch(
    sz, step, per, blob_ref, band_ref, shift_ref, amp_ref, rate_ref, pixel_ref, weight_ref,
    col_ref, row_ref, line_ref, result_ref,
):
    height = pixel_ref.shape[1]
    eight = (HALF, LANES)
    shape = (SLOTS, LANES)
    lane = iota(eight, 1)
    sub = iota(eight, 0)
    sub_f = sub.astype(jnp.float32)
    lane_f = lane.astype(jnp.float32)
    slots_all = COMPS * SLOTS
    width = COMPS * HALF
    keep = (iota(shape, 1) % HALF == iota(shape, 0) % HALF) & (iota(shape, 1) < 3 * width)
    keep = jnp.where(keep, 1.0, 0.0).astype(jnp.bfloat16)
    comp = lane // SLOTS % COMPS
    high_part = (lane < width) | (lane >= 2 * width)
    half_index = lane // HALF % COMPS * SLOTS + lane % HALF
    seat_a = lane // HALF == sub
    seat_b = lane // HALF == sub + HALF
    blank = jnp.zeros((LANES - 3 * width, LANES), jnp.float32)
    zero_tail = jnp.zeros((slots_all, LANES), jnp.bfloat16)
    zero_rows = jnp.zeros((LANES - 2 * slots_all, LANES), jnp.bfloat16)
    pending = []

    for slot in range(per):
        tile = step * per + slot
        blob = blob_ref[0, tile]
        zone = lax.div(blob, sz.blobs)
        local = lax.rem(blob, sz.blobs)
        rate = [rate_ref[g, tile] for g in range(COMPS)]
        amp = [amp_ref[g, tile] for g in range(COMPS)]
        row_rate = jnp.where(comp == 0, rate[0], jnp.where(comp == 1, rate[1], rate[2]))
        row_amp = jnp.where(comp == 0, amp[0], jnp.where(comp == 1, amp[1], amp[2]))
        row_shift = shift_ref[0, tile]
        row_base = row_shift + spread_rows(row_ref[pl.ds(blob, 1), :], eight)
        col_base = shift_ref[1, tile]
        col_table = col_ref[zone]
        square = []
        for half in range(2):
            index = jnp.full(eight, half * sz.blobs, jnp.int32) + local
            away = lane_f - col_base - take(col_table, index)
            square.append(away * away)
        cols = [[jnp.exp2(rate[g] * square[half]) for half in range(2)] for g in range(COMPS)]
        heads, tails, heads_f, tails_f = [], [], [], []
        for g in range(COMPS):
            both = jnp.concatenate(cols[g], axis=0)
            head = both.astype(jnp.bfloat16)
            head_f = head.astype(jnp.float32)
            heads.append(head)
            heads_f.append(head_f)
            tails_f.append(both - head_f)
            tails.append(tails_f[-1].astype(jnp.bfloat16))
        rights = []
        for half in range(2):
            span = slice(half * HALF, (half + 1) * HALF)
            top = [h[span] for h in heads_f]
            rights.append(
                jnp.concatenate(top + top + [t[span] for t in tails_f] + [blank], axis=0).astype(
                    jnp.bfloat16
                )
            )
        rows = []
        for part in range(height // 8):
            away = (sub_f + 8.0 * part) - row_base
            value = jnp.exp2(row_rate * (away * away)) * row_amp
            rows.append(value)
            line_ref[slot, 0, part * 8 : (part + 1) * 8, :] = value
            for half in range(2):
                seen = take(value, half_index + half * HALF)
                head = seen.astype(jnp.bfloat16).astype(jnp.float32)
                line_ref[slot, 1 + half, part * 8 : (part + 1) * 8, :] = jnp.where(
                    high_part, head, seen - head
                )
        models = []
        for half in range(2):
            left = []
            for i in range(0, height, 2):
                pair = jnp.concatenate(
                    [
                        spread_rows(line_ref[slot, 1 + half, i + d : i + d + 1, :], eight)
                        for d in range(2)
                    ],
                    axis=0,
                )
                left.append(pair.astype(jnp.bfloat16) * keep)
            models.append(
                lax.dot_general(
                    jnp.concatenate(left, axis=0), rights[half], (((1,), (0,)), ((), ())),
                    preferred_element_type=jnp.float32,
                )
            )
        heads_left = []
        tails_left = []
        for i in range(height):
            span = slice(i * HALF, (i + 1) * HALF)
            weight = spread_rows(weight_ref[tile, i : i + 1, :], shape)
            scaled = jnp.concatenate([models[0][span], models[1][span]], axis=0) * weight
            head, tail = split(scaled)
            heads_left.append(head)
            tails_left.append(tail)
        head, tail = split(weight_ref[tile] * pixel_ref[tile])
        heads_left.append(head)
        tails_left.append(tail)
        top = jnp.concatenate(heads, axis=0)
        low = jnp.concatenate(tails, axis=0)
        pending.append((tile, blob, local, slot, rows, heads_left, tails_left, top, low))
        if len(pending) < 2:
            continue
        left = [
            jnp.concatenate([pending[0][5][i], pending[1][5][i], pending[0][6][i], pending[1][6][i]], axis=1)
            for i in range(height + 1)
        ]
        zero = zero_tail
        right = jnp.concatenate(
            [
                jnp.concatenate([pending[0][7], zero, pending[0][7], zero], axis=1),
                jnp.concatenate([pending[0][8], zero, zero, zero], axis=1),
                jnp.concatenate([zero_rows] * 4, axis=1),
                jnp.concatenate([zero, pending[1][7], zero, pending[1][7]], axis=1),
                jnp.concatenate([zero, pending[1][8], zero, zero], axis=1),
                jnp.concatenate([zero_rows] * 4, axis=1),
            ],
            axis=0,
        )
        product = lax.dot_general(
            jnp.concatenate(left, axis=0), right, (((1,), (1,)), ((), ())),
            preferred_element_type=jnp.float32,
        )
        for member in range(2):
            tile, blob, local, held, rows = pending[member][:5]
            side = slice(member * LANES, (member + 1) * LANES)
            normal = None
            for i in range(height):
                line = spread_rows(line_ref[held, 0, i : i + 1, :], shape)
                term = product[i * SLOTS : (i + 1) * SLOTS, side] * line
                normal = term if normal is None else normal + term
            vector = None
            for part in range(height // 8):
                at = height * SLOTS + part * 8
                term = product[at : at + 8, side] * rows[part]
                vector = term if vector is None else vector + term
            folded = jnp.concatenate([normal, vector], axis=0)
            for shift in (LANES // 2, LANES // 4, LANES // 8):
                folded = folded + pltpu.roll(folded, shift, 1)
            upper, lower, vector = folded[:HALF], folded[HALF:SLOTS], folded[SLOTS:]
            step_back = SLOTS - HALF - 1
            main = jnp.where(
                seat_a, pltpu.roll(upper, 0, 1, stride=step_back, stride_axis=0),
                jnp.where(
                    seat_b,
                    pltpu.roll(lower, HALF * step_back, 1, stride=step_back, stride_axis=0), 0.0,
                ),
            )
            code = (
                lax.div(local, sz.share) * sz.systems
                + band_ref[0, tile] * sz.share
                + lax.rem(local, sz.share)
            )
            rest = jnp.where(lane == sub, pltpu.roll(upper, HALF, 1), 0.0)
            rest = jnp.where((lane >= SLOTS) & (lane < 2 * SLOTS), vector, rest)
            rest = jnp.where((lane == HALF) & (sub == 0), code.astype(jnp.float32), rest)
            result_ref[0, pl.ds(tile, 1), :] = jnp.sum(main, axis=0, keepdims=True)
            result_ref[1, pl.ds(tile, 1), :] = jnp.sum(rest, axis=0, keepdims=True)
        pending = []


def plan_route(sz, blob_ref, hit_ref):
    square = (sz.tiles, sz.tiles)
    zone = spread_rows(lax.div(blob_ref[...], sz.blobs).astype(jnp.float32), square)
    same = (zone == zone.T) & (iota(square, 0) < iota(square, 1))
    rank = jnp.sum(jnp.where(same, 1.0, 0.0), axis=0, keepdims=True)
    place = zone[:1] * float(sz.capacity) + rank
    entry = iota((sz.entries, sz.tiles), 0).astype(jnp.float32)
    hit_ref[...] = jnp.where(entry == place, 1.0, 0.0).astype(jnp.bfloat16)


def route_terms(sz, hit_ref, result_ref, terms_ref):
    hit = hit_ref[...]
    left = jnp.concatenate([result_ref[0], result_ref[1]], axis=1)
    moved = None
    for _ in range(3):
        piece = left.astype(jnp.bfloat16)
        left = left - piece.astype(jnp.float32)
        part = lax.dot_general(
            hit, piece, (((1,), (0,)), ((), ())), preferred_element_type=jnp.float32
        )
        moved = part if moved is None else moved + part
    for number in range(sz.zones):
        start = number * sz.capacity
        terms_ref[number, : sz.capacity, :] = moved[start : start + sz.capacity, :LANES]
        total = None
        for seat in range(SEATS):
            at = start + seat * sz.rest
            piece = moved[at : at + sz.rest, LANES:]
            piece = pltpu.roll(piece, seat * SEAT, 1) if seat else piece
            total = piece if total is None else total + piece
        terms_ref[number, sz.capacity : sz.capacity + sz.rest, :] = total


def find_seats(sz, zone, cat_ref, edge_ref, seat_ref):
    shape = (HALF, LANES)
    edges = spread_rows(edge_ref[...], shape)
    source = iota((sz.sources, LANES), 0)
    lane = iota((1, LANES), 1)
    total = None
    for side in range(3):
        near = lax.rem(zone + side - 1 + sz.zones, sz.zones)
        member = cat_ref[near, sz.member_row : sz.member_row + HALF, :].astype(jnp.int32)
        top = sz.edge + sz.sources
        if side == 0:
            valid = (member >= top) & (zone > 0)
            target = take(edges, jnp.where(valid, member - top, 0))
        elif side == 1:
            valid = (member >= sz.edge) & (member < top)
            target = member - sz.edge
        else:
            valid = (member >= 0) & (member < sz.edge) & (zone < sz.zones - 1)
            target = take(edges, jnp.where(valid, member + sz.edge, 0))
        target = jnp.where(valid, target, -1)
        for row in range(HALF):
            hit = source == target[row : row + 1, :]
            right = jnp.where(hit, 1.0, 0.0).astype(jnp.bfloat16)
            slot = side * SLOTS + row + lane // sz.blobs * HALF
            left = jnp.concatenate(
                [slot, lane % sz.blobs, jnp.zeros((SLOTS - 2, LANES), jnp.int32)], axis=0
            )
            part = lax.dot_general(
                left.astype(jnp.float32).astype(jnp.bfloat16), right, (((1,), (1,)), ((), ())),
                preferred_element_type=jnp.float32,
            )
            total = part if total is None else total + part
    seat_ref[...] = total[:8].astype(jnp.int32)


def gather_terms(sz, got_ref, table_ref, part_ref):
    for zone in range(sz.zones):
        start = zone * sz.capacity
        table_ref[start : start + sz.capacity, :LANES] = got_ref[zone, : sz.capacity, :]
        rest = got_ref[zone, sz.capacity : sz.capacity + sz.rest, :]
        for seat in range(SEATS):
            at = start + seat * sz.rest
            table_ref[at : at + sz.rest, LANES:] = (
                pltpu.roll(rest, LANES - seat * SEAT, 1) if seat else rest
            )
    square = (LANES, LANES)
    diagonal = iota(square, 0) == iota(square, 1)
    codes = []
    for at in range(0, sz.entries, LANES):
        block = table_ref[at : at + LANES, LANES:]
        code = take(block, jnp.full(square, HALF, jnp.int32))
        codes.append(jnp.sum(jnp.where(diagonal, code, 0.0), axis=0, keepdims=True))
    codes = jnp.concatenate(codes, axis=1)
    count = sz.bands * sz.block
    system = iota((count, sz.entries), 0)
    hit = jnp.where(system.astype(jnp.float32) == codes, 1.0, 0.0).astype(jnp.bfloat16)
    head, tail = split(table_ref[...])
    dims = (((1,), (0,)), ((), ()))
    total = lax.dot_general(hit, head, dims, preferred_element_type=jnp.float32)
    total = total + lax.dot_general(hit, tail, dims, preferred_element_type=jnp.float32)
    lane = iota((sz.third, LANES), 1) // SEAT
    for owner in range(sz.bands):
        start = owner * sz.block
        part_ref[owner, : sz.block, :] = total[start : start + sz.block, :LANES]
        rest = None
        for seat in range(FILTER_BANDS):
            at = start + seat * sz.third
            piece = total[at : at + sz.third, LANES:]
            piece = jnp.where(lane == seat, pltpu.roll(piece, seat * SEAT, 1) if seat else piece, 0.0)
            rest = piece if rest is None else rest + piece
        part_ref[owner, sz.block :, :] = rest


def solve(sz, summed, flat_ref, square_ref):
    main, rest = summed[: sz.block], summed[sz.block :]
    rest = jnp.concatenate(
        [pltpu.roll(rest, LANES - s * SEAT, 1) if s else rest for s in range(FILTER_BANDS)], axis=0
    )
    fill = jnp.zeros((LANES - sz.block, LANES), jnp.float32)
    flat_ref[:LANES, :] = jnp.concatenate([main, fill], axis=0).T
    flat_ref[LANES:, :] = jnp.concatenate([rest, fill], axis=0).T[: 2 * SLOTS]
    for l in range(SLOTS):
        for j in range(SLOTS):
            if (l - j) % SLOTS == HALF:
                at = LANES + min(j, l)
                square_ref[l, j : j + 1, :] = flat_ref[at : at + 1, :]
        for low, high, row in (
            (max(0, l - HALF + 1), l + 1, lambda j: HALF * j + l - j),
            (l + HALF + 1, SLOTS, lambda j: HALF * j + SLOTS + l - j),
        ):
            if low < high:
                square_ref[l, low:high, :] = flat_ref[pl.ds(row(low), high - low, stride=HALF - 1), :]
        for low, high, row in (
            (l + 1, min(l + HALF, SLOTS), lambda j: HALF * l + j - l),
            (0, l - HALF, lambda j: HALF * l + SLOTS + j - l),
        ):
            if low < high:
                square_ref[l, low:high, :] = flat_ref[row(low) : row(low) + high - low, :]
    shape = (SLOTS, LANES)
    sub = iota(shape, 0)
    columns = [square_ref[l] + jnp.where(sub == l, PRIOR, 0.0) for l in range(SLOTS)]
    columns.append(flat_ref[LANES + SLOTS : LANES + 2 * SLOTS, :])
    scale = columns[0]
    for k in range(SLOTS):
        column = columns[k]
        inverse = 1.0 / column[k : k + 1]
        scale = jnp.where(sub == k, column, scale)
        column = jnp.where(sub == k, 0.0, column)
        for l in range(k + 1, SLOTS + 1):
            ratio = columns[l][k : k + 1] * inverse
            columns[l] = columns[l] - column * ratio
    return columns[SLOTS] / scale


def whole_kernel(
    sz, per,
    pixel_hbm, weight_hbm, blob_hbm, band_hbm, shift_hbm, amp_hbm, sigma_hbm,
    source_hbm, edge_hbm, member_hbm, count_hbm, out_ref,
    blob_ref, band_ref, shift_ref, amp_ref, sigma_ref, blob_row_ref,
    source_ref, edge_ref, member_ref, count_ref, pixel_ref, weight_ref, rate_row_ref, rate_ref, pack_ref, cat_ref,
    stage_ref, turned_ref, col_ref, row_ref, line_ref, result_ref, hit_ref, terms_ref,
    got_ref, table_ref, part_ref, sum_ref, flat_ref, square_ref, solved_ref, flux_ref, seat_ref,
    load_sem, send_cat, recv_cat, own_cat,
    send_term, recv_term, own_term, send_sum, recv_sum, send_flux, recv_flux,
):
    zones, bands = sz.zones, sz.bands
    zone = lax.axis_index("zone")
    band = lax.axis_index("band")
    at = lambda dz, db: (lax.rem(zone + dz + zones, zones), lax.rem(band + db, bands))
    far = [(partner(zone, step, zones), band) for step in range(zones - 1, 0, -1)]
    near = [at(0, db) for db in range(1, bands)]
    above, below = zone < zones - 1, zone > 0
    beside = [(1, above, below), (-1, below, above)]
    barrier = pltpu.get_barrier_semaphore()

    def greet(target):
        pl.semaphore_signal(barrier, inc=1, device_id=target, device_id_type=MESH)

    for target in far + near:
        greet(target)
    for dz, sends, _ in beside:

        @pl.when(sends)
        def _():
            for db in range(1, bands):
                greet(at(dz, db))

    pairs = [
        (source_hbm, source_ref), (edge_hbm, edge_ref), (member_hbm, member_ref),
        (count_hbm, count_ref), (sigma_hbm, sigma_ref), (blob_hbm, blob_ref),
        (blob_hbm, blob_row_ref), (band_hbm, band_ref), (shift_hbm, shift_ref),
        (amp_hbm, amp_ref), (pixel_hbm, pixel_ref), (weight_hbm, weight_ref),
    ]
    loads = [
        pltpu.make_async_copy(source, target, load_sem.at[number])
        for number, (source, target) in enumerate(pairs)
    ]
    for copy in loads:
        copy.start()
    for copy in loads[:5]:
        copy.wait()
    loads = loads[5:]
    sigma = sigma_ref[...]
    rate_row_ref[...] = (-0.5 * LOG2E) / (sigma * sigma)
    pack_catalog(sz, source_ref, edge_ref, member_ref, count_ref, pack_ref)
    loads.append(pltpu.make_async_copy(rate_row_ref, rate_ref, load_sem.at[len(pairs)]))
    loads[-1].start()
    sent = pl.ds(0, sz.sent_rows)
    own = pltpu.make_async_copy(pack_ref.at[sent], cat_ref.at[zone, sent], own_cat)
    own.start()
    ends = lax.div(zone, zones - 1) + lax.div(zones - 1 - zone, zones - 1)
    pl.semaphore_wait(barrier, len(far) + len(near) + (bands - 1) * (2 - ends))
    copies = []
    for order, target in enumerate(far):
        copy = pltpu.make_async_remote_copy(
            src_ref=pack_ref.at[sent],
            dst_ref=cat_ref.at[zone, sent],
            send_sem=send_cat.at[order],
            recv_sem=recv_cat.at[order],
            device_id=target,
            device_id_type=MESH,
        )
        copy.start()
        copies.append(copy)
    for copy in loads:
        copy.wait()
    plan_route(sz, blob_row_ref, hit_ref)
    own.wait()
    for copy in copies:
        copy.wait()
    prepare(sz, cat_ref, stage_ref, turned_ref, col_ref, row_ref)

    def body(step, carry):
        tile_batch(
            sz, step, per, blob_ref, band_ref, shift_ref, amp_ref, rate_ref,
            pixel_ref, weight_ref, col_ref, row_ref, line_ref, result_ref,
        )
        return carry

    lax.fori_loop(0, sz.tiles // per, body, 0)
    route_terms(sz, hit_ref, result_ref, terms_ref)
    own = pltpu.make_async_copy(terms_ref.at[zone], got_ref.at[zone], own_term)
    own.start()
    copies = []
    for order, target in enumerate(far):
        copy = pltpu.make_async_remote_copy(
            src_ref=terms_ref.at[target[0]],
            dst_ref=got_ref.at[zone],
            send_sem=send_term.at[order],
            recv_sem=recv_term.at[order],
            device_id=target,
            device_id_type=MESH,
        )
        copy.start()
        copies.append(copy)
    find_seats(sz, zone, cat_ref, edge_ref, seat_ref)
    own.wait()
    for copy in copies:
        copy.wait()

    gather_terms(sz, got_ref, table_ref, part_ref)
    copies = []
    for order, target in enumerate(near):
        copy = pltpu.make_async_remote_copy(
            src_ref=part_ref.at[target[1]],
            dst_ref=sum_ref.at[order],
            send_sem=send_sum.at[order],
            recv_sem=recv_sum.at[order],
            device_id=target,
            device_id_type=MESH,
        )
        copy.start()
        copies.append(copy)
    for copy in copies:
        copy.wait()
    summed = part_ref[band]
    for order in range(len(near)):
        summed = summed + sum_ref[order]
    solved = solve(sz, summed, flat_ref, square_ref)
    eight = (HALF, LANES)
    packed = jnp.where(
        iota(eight, 1) < LANES // 2, solved[:HALF], pltpu.roll(solved[HALF:], LANES // 2, 1)
    )
    solved_ref[...] = packed
    flux_ref[bands + band] = packed

    def flux_copy(order, side, target):
        return pltpu.make_async_remote_copy(
            src_ref=solved_ref,
            dst_ref=flux_ref.at[side * bands + band],
            send_sem=send_flux.at[order],
            recv_sem=recv_flux.at[order],
            device_id=target,
            device_id_type=MESH,
        )

    across = []
    for number, (dz, sends, receives) in enumerate(beside):
        first = bands - 1 + number * bands
        group = [flux_copy(first + db, 1 - dz, at(dz, db)) for db in range(bands)]
        across.append((group, sends, receives))

        @pl.when(sends)
        def _():
            for copy in group:
                copy.start()

    copies = [flux_copy(order, 1, target) for order, target in enumerate(near)]
    for copy in copies:
        copy.start()
    for copy in copies:
        copy.wait()
    for group, sends, receives in across:

        @pl.when(sends)
        def _():
            for copy in group:
                copy.wait_send()

        @pl.when(receives)
        def _():
            for copy in group:
                copy.wait_recv()

    sub = iota(eight, 0)
    for part in range(sz.parts):
        span = slice(part * LANES, (part + 1) * LANES)
        slot = spread_rows(seat_ref[0:1, span], eight)
        blob = spread_rows(seat_ref[1:2, span], eight)
        row = slot % SLOTS
        key = slot // SLOTS * bands + blob // sz.share
        index = row // HALF * (LANES // 2) + blob % sz.share
        key = jnp.where(sub == row % HALF, key, -1)
        values = [jnp.zeros(eight, jnp.float32) for _ in range(FILTER_BANDS)]
        for table in range(3 * bands):
            flux = flux_ref[table]
            hit = key == table
            for k in range(FILTER_BANDS):
                values[k] = jnp.where(hit, take(flux, index + k * sz.share), values[k])
        out_ref[:, span] = jnp.concatenate(
            [jnp.sum(value, axis=0, keepdims=True) for value in values], axis=0
        )


def on_device(
    sizes, pixels, inv_var, tile_offset, psf_amp, psf_sigma, tile_blob, tile_band,
    source_pos, edge_rows, blob_members, sources_per_blob,
):
    zones, bands = sizes
    sz = Sizes(
        zones, bands, source_pos.shape[1], edge_rows.shape[0] // 2,
        sources_per_blob.shape[0], pixels.shape[0],
    )
    dma = pltpu.SemaphoreType.DMA
    f32 = jnp.float32
    tiles, height, width = pixels.shape
    per = TILES_STEP
    while tiles % per:
        per -= 1
    turned = -(-zones * HALF // LANES)
    near = 3 * bands - 1
    rows = sz.block + sz.third
    blob_row = tile_blob.reshape(1, -1)
    return pl.pallas_call(
        functools.partial(whole_kernel, sz, per),
        out_shape=jax.ShapeDtypeStruct((FILTER_BANDS, sz.sources), f32),
        in_specs=[ANY] * 11,
        out_specs=VMEM,
        scratch_shapes=[
            pltpu.SMEM((1, tiles), jnp.int32),
            pltpu.SMEM((1, tiles), jnp.int32),
            pltpu.SMEM((2, tiles), f32),
            pltpu.SMEM((COMPS, tiles), f32),
            pltpu.VMEM((COMPS, tiles), f32),
            pltpu.VMEM((1, tiles), jnp.int32),
            pltpu.VMEM((2, sz.sources), f32),
            pltpu.VMEM((1, 2 * sz.edge), jnp.int32),
            pltpu.VMEM((SLOTS, sz.blobs), jnp.int32),
            pltpu.VMEM((1, sz.blobs), jnp.int32),
            pltpu.VMEM((tiles, height, width), f32),
            pltpu.VMEM((tiles, height, width), f32),
            pltpu.VMEM((COMPS, tiles), f32),
            pltpu.SMEM((COMPS, tiles), f32),
            pltpu.VMEM((sz.cat_rows, LANES), f32),
            pltpu.VMEM((zones, sz.cat_rows, LANES), f32),
            pltpu.VMEM((turned * LANES, LANES), f32),
            pltpu.VMEM((turned, LANES, LANES), f32),
            pltpu.VMEM((zones, HALF, LANES), f32),
            pltpu.VMEM((zones * sz.blobs, LANES), f32),
            pltpu.VMEM((per, 3, height, width), f32),
            pltpu.VMEM((2, tiles, LANES), f32),
            pltpu.VMEM((sz.entries, tiles), jnp.bfloat16),
            pltpu.VMEM((zones, sz.rows, LANES), f32),
            pltpu.VMEM((zones, sz.rows, LANES), f32),
            pltpu.VMEM((sz.entries, 2 * LANES), f32),
            pltpu.VMEM((bands, rows, LANES), f32),
            pltpu.VMEM((bands - 1, rows, LANES), f32),
            pltpu.VMEM((LANES + 2 * SLOTS, LANES), f32),
            pltpu.VMEM((SLOTS, SLOTS, LANES), f32),
            pltpu.VMEM((HALF, LANES), f32),
            pltpu.VMEM((3 * bands, HALF, LANES), f32),
            pltpu.VMEM((8, sz.sources), jnp.int32),
            dma((13,)), dma((zones - 1,)), dma((zones - 1,)), dma,
            dma((zones - 1,)), dma((zones - 1,)), dma,
            dma((bands - 1,)), dma((bands - 1,)),
            dma((near,)), dma((near,)),
        ],
        compiler_params=pltpu.CompilerParams(
            collective_id=0, has_side_effects=True,
        ),
    )(
        pixels, inv_var, blob_row, tile_band.reshape(1, -1), tile_offset, psf_amp, psf_sigma,
        source_pos, edge_rows.reshape(1, -1), blob_members.T,
        sources_per_blob.reshape(1, -1),
    )


def solution(mesh):
    sizes = (mesh.shape["zone"], mesh.shape["band"])
    return jax.shard_map(
        functools.partial(on_device, sizes),
        mesh=mesh,
        in_specs=(
            P(("zone", "band"), None, None),
            P(("zone", "band"), None, None),
            P(None, ("zone", "band")),
            P(None, ("zone", "band")),
            P(None, ("zone", "band")),
            P(("zone", "band")),
            P(("zone", "band")),
            P(None, "zone"),
            P("zone"),
            P("zone", None),
            P("zone"),
        ),
        out_specs=P(None, "zone"),
        check_vma=False,
    )
```
